32 devices in a mesh: row: 16 (over z, y, core), rep: 2 (over x).
Axes of the slice: x: 2, y: 2, z: 4, core: 2. Of those that a mesh axis runs over, the one named last changes fastest.
Arguments:
- features: bfloat16 [8192, 128], P('row'), may hold values from -6 to 6
- input_weight: bfloat16 [128, 512], replicated, may hold values from -5 to 5
- output_weight: bfloat16 [512, 512], replicated, may hold values from -0.25 to 0.25
- cotangent: bfloat16 [8192, 512], P(('row', 'rep')), may hold values from -0.25 to 0.25
- adjacency_tiles: bfloat16 [64, 8, 128, 128], P('row', 'rep'), may hold values from 0.0009994507 to 1
- block_columns: int32 [64, 8], P('row', 'rep'), may hold values from 0 to 63, as said below
- graph_sizes: int32 [16], replicated, may hold values from 1 to 2048, 8192 in all
Outputs:
- scores: bfloat16 [8192, 512], P(('row', 'rep'))
- grad_input: float32 [128, 512], replicated
- grad_output: float32 [512, 512], replicated
The draws below stay inside these ranges and needn't reach their ends.
Inputs may be any that keep to these rules, and one draw needn't show every extreme that they name: `block_columns`: each row block b lists 8 distinct column blocks, its own first, every one within 12 blocks of b along the closed loop of 64 blocks (indices taken mod 64); row block 0 lists the blocks at both ends of that reach. `graph_sizes`: the sizes sum to 8192.
All inputs are finite; a program needn't handle non-finite values.
Results may differ from the reference program's by a relative error of at most 0.0045.
The reference program's roundings to bfloat16 on the way (of `masked`, `first`, `hidden`, `second`, `scaled` and `delta`) count: a program that leaves them out, or rounds other values in their place, can miss the bound.
Values may be sent and summed in bfloat16 or wider, within the bound.
A program may use at most 64 MiB of HBM per device.

```python
import math
import jax
import jax.numpy as jnp
import numpy as np
from jax import lax

TILE = 128
F_IN = 128
HID = 512
RB = 4
HOPS = 3
KT = 8
NBLK = 64
NODES = 8192
GRAPHS = 16


def draw_block_columns(key, part):
    reach = HOPS * RB
    offsets = jnp.concatenate([jnp.arange(-reach, 0), jnp.arange(1, reach + 1)]).astype(jnp.int32)
    raw = jax.random.randint(key, (NBLK, 2 * reach), 0, 2 ** 20)
    scores = raw * (2 * reach) + jnp.arange(2 * reach, dtype=jnp.int32)[None, :]
    forced = (jnp.arange(NBLK)[:, None] == 0) & (jnp.abs(offsets)[None, :] == reach)
    scores = jnp.where(forced, jnp.arange(2 * reach, dtype=jnp.int32)[None, :] - 4 * reach, scores)
    order = jnp.argsort(scores, axis=1)[:, :KT - 1]
    chosen = offsets[order]
    shifts = jnp.concatenate([jnp.zeros((NBLK, 1), jnp.int32), chosen], axis=1)
    return ((jnp.arange(NBLK, dtype=jnp.int32)[:, None] + shifts) % NBLK).astype(jnp.int32)


def raised(values, stream_key, source, target, blocks, factor):
    owner, partner = [(jnp.arange(values.shape[position]) // (values.shape[position] // blocks)).reshape([-1 if axis == position else 1 for axis in range(values.ndim)]) for position in (source, target)]
    chosen = jax.random.permutation(stream_key, blocks)[partner]
    strong = (owner == chosen) | (owner == (partner + blocks // 2) % blocks)
    return jnp.where(strong, factor * values, values)


def block_levels(stream_key, extent, cuts, least, largest):
    gain = 1.0
    for dim, parts in cuts:
        heights = jax.random.uniform(jax.random.fold_in(jax.random.fold_in(stream_key, 6), dim), (parts,), jnp.float32, least / len(cuts), largest / len(cuts))
        gain = gain * jnp.repeat(jnp.exp(heights), extent[dim] // parts).reshape((-1,) + (1,) * (len(extent) - 1 - dim))
    return gain


def profile(count, total, limit, skew):
    weights = [(1 << 20) // math.isqrt(standing ** skew) + 1 for standing in range(2, count + 1)]
    surplus, holding = total - limit - (count - 1), [1] * (count - 1)
    while surplus > 0:
        movable = [i for i in range(count - 1) if holding[i] < limit]
        mass, remaining = sum([weights[i] for i in movable]), surplus
        for i in movable:
            addition = min(limit - holding[i], max(1, remaining * weights[i] // mass), surplus)
            holding[i] = holding[i] + addition
            surplus = surplus - addition
    return np.array([limit] + holding)


def uneven(stream_key, number_of, total, most, slope):
    if number_of == 2:
        one = jax.random.randint(stream_key, (), max(1, total - most), min(most, total - 1) + 1)
        return jnp.stack([one, total - one])
    lengths = jnp.asarray(profile(number_of, total, most, slope), jnp.int32)
    twos = (number_of - 1) // 2
    donor, receiver = lengths[1:1 + 2 * twos:2], lengths[2:2 + 2 * twos:2]
    room = jnp.minimum(donor - 1, most - receiver)
    shifted = jax.random.randint(jax.random.fold_in(stream_key, 1), (twos,), 0, 1 << 20) % (room + 1)
    lengths = lengths.at[1:1 + 2 * twos:2].set(donor - shifted).at[2:2 + 2 * twos:2].set(receiver + shifted)
    return lengths[jax.random.permutation(jax.random.fold_in(stream_key, 2), number_of)]


def noise(rng, extent, scale, limit, shards=(), kind=jnp.bfloat16):
    entries = scale * jax.random.normal(rng, extent, jnp.float32)
    if shards:
        entries = entries * block_levels(rng, extent, shards, -0.22, 0.18)
    return jnp.clip(entries, -limit, limit).astype(kind)


def bell_draw_with(own_key, dims, spread, bound, split, heavy, kind=jnp.bfloat16):
    result = spread * jax.random.normal(own_key, dims, jnp.float32)
    if split:
        result = result * block_levels(own_key, dims, split, -0.22, 0.18)
    return jnp.clip(raised(result, jax.random.fold_in(own_key, 3), *heavy), -bound, bound).astype(kind)


def setup_inputs(seed: int = 0) -> dict:
    arg_keys = jax.random.split(jax.random.key(seed), 8)
    return {
        "features": noise(arg_keys[0], (NODES, F_IN), 1.0, 6.0, ((0, 16),)),
        "input_weight": noise(arg_keys[1], (F_IN, HID), 1.0, 5.0),
        "output_weight": noise(arg_keys[2], (HID, HID), HID ** -0.5, 0.25),
        "cotangent": bell_draw_with(arg_keys[3], (NODES, HID), 0.01, 0.25, ((0, 32),), (0, 1, 32, 2.75)),
        "adjacency_tiles": jnp.clip(jnp.exp(math.log(1.0) - 6.9083047 * jax.random.uniform(arg_keys[4], (NBLK, KT, TILE, TILE), jnp.float32) ** block_levels(arg_keys[4], (NBLK, KT, TILE, TILE), ((0, 16), (1, 2)), -0.2, 0.2)), 0.0009994507, 1.0).astype(jnp.bfloat16),
        "block_columns": draw_block_columns(jax.random.fold_in(arg_keys[7], 71), 0),
        "graph_sizes": uneven(arg_keys[6], GRAPHS, NODES, 16 * TILE, 2).astype(jnp.int32),
    }


def graph_of(nodes, ends):
    return lax.optimization_barrier(jnp.sum((nodes[..., None] >= ends).astype(jnp.int32), axis=-1))

def reference(features, input_weight, output_weight, cotangent, adjacency_tiles, block_columns, graph_sizes):
    ends = jnp.cumsum(graph_sizes).astype(jnp.int32)
    blocks = adjacency_tiles.shape[0]
    tile = adjacency_tiles.shape[2]
    within = jnp.arange(tile, dtype=jnp.int32)
    row_ids = graph_of(jnp.arange(blocks, dtype=jnp.int32)[:, None] * tile + within, ends)
    col_ids = graph_of(block_columns[..., None] * tile + within, ends)
    same = row_ids[:, None, :, None] == col_ids[:, :, None, :]
    masked = jnp.where(same, adjacency_tiles, jnp.zeros_like(adjacency_tiles))
    degree = 1.0 + lax.optimization_barrier(jnp.sum(masked.astype(jnp.float32), axis=(1, 3))).reshape(-1)

    def aggregate(values):
        grid = values.reshape(blocks, tile, -1)

        def single(pair):
            tiles_here, columns_here = pair
            return jnp.einsum('kij,kjf->if', tiles_here.astype(jnp.float32), grid[columns_here], precision=lax.Precision.HIGHEST)
        return lax.map(single, (masked, block_columns)).reshape(blocks * tile, -1)
    feats = features.astype(jnp.float32)
    first = ((aggregate(feats) + feats) / degree[:, None]).astype(jnp.bfloat16)
    preact = jnp.dot(first, input_weight, preferred_element_type=jnp.float32)
    hidden = jnp.maximum(preact, 0.0).astype(jnp.bfloat16)
    hidden_wide = hidden.astype(jnp.float32)
    second = ((aggregate(hidden_wide) + hidden_wide) / degree[:, None]).astype(jnp.bfloat16)
    scores = jnp.dot(second, output_weight, preferred_element_type=jnp.float32).astype(jnp.bfloat16)
    grad_output = jnp.dot(second.T, cotangent, preferred_element_type=jnp.float32)
    scaled = (jnp.dot(cotangent, output_weight.T, preferred_element_type=jnp.float32) / degree[:, None]).astype(jnp.bfloat16)
    unused, pullback = jax.vjp(aggregate, hidden_wide)
    transposed, = pullback(scaled.astype(jnp.float32))
    back = transposed + scaled.astype(jnp.float32)
    delta = jnp.where(preact > 0.0, back, 0.0).astype(jnp.bfloat16)
    grad_input = jnp.dot(first.T, delta, preferred_element_type=jnp.float32)
    return (scores, grad_input, grad_output)
```

```python
import functools

import jax
import jax.numpy as jnp
from jax import lax
from jax.experimental import pallas as pl
from jax.experimental.pallas import tpu as pltpu
from jax.sharding import PartitionSpec as P

HOPS = 3
SPAN = 2 * HOPS + 1
SHIFTS = [s for s in range(-HOPS, HOPS + 1) if s]
MESH = pl.DeviceIdType.MESH
ANY = pl.BlockSpec(memory_space=pl.ANY)
VMEM = pl.BlockSpec(memory_space=pltpu.VMEM)
SMEM = pl.BlockSpec(memory_space=pltpu.SMEM)
F32 = jnp.float32
BF16 = jnp.bfloat16


def dot(a, b, dims):
    return lax.dot_general(a, b, ((dims[:1], dims[1:]), ((), ())), preferred_element_type=F32)


def greet(peers):
    barrier = pltpu.get_barrier_semaphore()
    for peer in peers:
        pl.semaphore_signal(barrier, inc=1, device_id=peer, device_id_type=MESH)
    pl.semaphore_wait(barrier, len(peers))


def remote(src, dst, send, recv, index, peer):
    return pltpu.make_async_remote_copy(
        src_ref=src, dst_ref=dst, send_sem=send.at[index], recv_sem=recv.at[index],
        device_id=peer, device_id_type=MESH,
    )


def open_kernel(rows, reps, feats, cot, tiles, cols, band, cots, all_tiles, all_cols, send, recv, local):
    row, rep = lax.axis_index("row"), lax.axis_index("rep")
    near = [(lax.rem(row + s + rows, rows), rep) for s in SHIFTS]
    others = [(row, lax.rem(rep + t, reps)) for t in range(1, reps)]
    greet(near + others)
    copies, n = [], 0
    pieces = ((tiles, all_tiles), (cols, all_cols), (cot, cots))
    for peer in others:
        for src, dst in pieces:
            copies.append(remote(src, dst.at[rep], send, recv, n, peer))
            n += 1
    for s, peer in zip(SHIFTS, near):
        copies.append(remote(feats, band.at[HOPS - s], send, recv, n, peer))
        n += 1
    for i, (src, dst) in enumerate(pieces):
        copies.append(pltpu.make_async_copy(src, dst.at[rep], local.at[i]))
    copies.append(pltpu.make_async_copy(feats, band.at[HOPS], local.at[3]))
    for copy in copies:
        copy.start()
    for copy in copies:
        copy.wait()


def front_kernel(rows, reps, blocks, tile, tiles, cols, row_ids, band_ids, band, cots, w1, w2,
                 dense, first_o, preact_o, hidden_o, scaled_o, terms_o, own_o, deg_o):
    row, rep = lax.axis_index("row"), lax.axis_index("rep")
    total = rows * blocks
    per = tiles.shape[2]
    dense[...] = jnp.zeros_like(dense)
    for b in range(blocks):
        at = pl.ds(b * tile, tile)
        ids = row_ids[at, :]
        sums = jnp.ones((tile, 1), F32)
        for j in range(reps):
            for k in range(per):
                slot = lax.rem(cols[j, b, k] + total - (row - HOPS) * blocks, total)
                same = ids == band_ids[pl.ds(slot, 1), :]
                value = jnp.where(same, tiles[j, b, k].astype(F32), 0.0)
                sums = sums + jnp.sum(value, axis=1, keepdims=True)
                dense[at, pl.ds(pl.multiple_of(slot * tile, tile), tile)] = value.astype(BF16)
        deg_o[at, :] = sums
    degree = deg_o[...]
    local = blocks * tile
    flat = band[...].reshape(SPAN * local, -1)
    summed = dot(dense[...], flat, (1, 0))
    first = ((summed + band[HOPS].astype(F32)) / degree).astype(BF16)
    first_o[...] = first
    half = w1.shape[1] // reps
    at = pl.ds(pl.multiple_of(rep * half, half), half)
    preact = dot(first, w1[:, at], (1, 0))
    preact_o[...] = preact
    hidden_o[...] = jnp.maximum(preact, 0.0).astype(BF16)
    pulled = dot(cots[...].reshape(local, -1), w2[at, :], (1, 1))
    scaled = (pulled / degree).astype(BF16)
    scaled_t = scaled.astype(F32).T.astype(BF16)
    for s in range(SPAN):
        part = dot(scaled_t, dense[:, s * local:(s + 1) * local], (1, 0))
        if s == HOPS:
            own_o[...] = part.T + scaled.astype(F32)
        terms_o[s] = part.astype(BF16)
    scaled_o[...] = scaled


def band_kernel(rows, hidden, terms, hid_band, term_band, send, recv, local):
    row, rep = lax.axis_index("row"), lax.axis_index("rep")
    near = [(lax.rem(row + s + rows, rows), rep) for s in SHIFTS]
    greet(near)
    copies, n = [], 0
    for s, peer in zip(SHIFTS, near):
        copies.append(remote(hidden, hid_band.at[HOPS - s], send, recv, n, peer))
        where = (HOPS - s) if s > 0 else (HOPS - s - 1)
        copies.append(remote(terms.at[HOPS + s], term_band.at[where], send, recv, n + 1, peer))
        n += 2
    copies.append(pltpu.make_async_copy(hidden, hid_band.at[HOPS], local.at[0]))
    for copy in copies:
        copy.start()
    for copy in copies:
        copy.wait()


def back_kernel(dense, hid_band, term_band, first, preact, own, deg, cots, second_o, grads_o):
    local, half = preact.shape
    summed = dot(dense[...], hid_band[...].reshape(SPAN * local, half), (1, 0))
    second = ((summed + hid_band[HOPS].astype(F32)) / deg[...]).astype(BF16)
    second_o[...] = second
    out = dot(second, cots[...].reshape(local, -1), (0, 0))
    width = out.shape[1] // half
    for i in range(width):
        grads_o[i * half:(i + 1) * half, :] = out[:, i * half:(i + 1) * half]
    got = term_band[0].astype(F32)
    for i in range(1, SPAN - 1):
        got = got + term_band[i].astype(F32)
    back = got.T + own[...]
    delta = jnp.where(preact[...] > 0.0, back, 0.0).astype(BF16)
    grads_o[width * half:, :] = dot(first[...], delta, (0, 0))


def swap_kernel(reps, second, full, send, recv, local):
    row, rep = lax.axis_index("row"), lax.axis_index("rep")
    others = [(row, lax.rem(rep + t, reps)) for t in range(1, reps)]
    greet(others)
    copies = [remote(second.at[peer[1]], full.at[rep], send, recv, n, peer) for n, peer in enumerate(others)]
    copies.append(pltpu.make_async_copy(second.at[rep], full.at[rep], local.at[0]))
    for copy in copies:
        copy.start()
    for copy in copies:
        copy.wait()


def sum_kernel(chips, reps, second, grads, full, whole, mine, pair, parts, send, recv, local):
    row, rep = lax.axis_index("row"), lax.axis_index("rep")
    chip, core = row // 2, lax.rem(row, 2)
    sibling = (chip * 2 + 1 - core, rep)
    turns = [lax.rem(chip + t, chips) for t in range(1, chips)]
    peers = [(q * 2 + core, rep) for q in turns]
    others = [(row, lax.rem(rep + t, reps)) for t in range(1, reps)]
    greet([sibling] + peers + others)
    a = remote(grads.at[1 - core], pair, send, recv, 0, sibling)
    a.start()
    early = [remote(second.at[peer[1]], full.at[rep], send, recv, 1 + n, peer) for n, peer in enumerate(others)]
    early.append(pltpu.make_async_copy(second.at[rep], full.at[rep], local.at[0]))
    for copy in early:
        copy.start()
    base = reps
    a.wait()
    mine[...] = grads[core] + pair[...]
    copies = [remote(mine.at[q], parts.at[t], send, recv, base + t, peer)
              for t, (q, peer) in enumerate(zip(turns, peers))]
    for copy in copies:
        copy.start()
    total = mine[chip]
    for t, copy in enumerate(copies):
        copy.wait_recv()
        total = total + parts[t]
    whole[rep, core, chip] = total
    base = base + chips - 1
    spread = [remote(whole.at[rep, core, chip], whole.at[rep, core, chip], send, recv, base + t, peer)
              for t, peer in enumerate(peers)]
    for copy in spread:
        copy.start()
    for copy in copies:
        copy.wait_send()
    for copy in spread:
        copy.wait()
    base = base + chips - 1
    block = whole.at[rep, core]
    last = [remote(block, block, send, recv, base + n, peer) for n, peer in enumerate(others)]
    base = base + reps - 1
    side = [remote(block, block, send, recv, base, sibling)]
    for copy in last + side:
        copy.start()
    for n, copy in enumerate(last):
        copy.wait_recv()
        came = whole.at[lax.rem(rep + reps - 1 - n, reps), core]
        step = remote(came, came, send, recv, base + 1 + n, sibling)
        step.start()
        side.append(step)
    for copy in last:
        copy.wait_send()
    for copy in side + early:
        copy.wait()


def params(number=None):
    limit = 48 << 20
    if number is None:
        return pltpu.CompilerParams(vmem_limit_bytes=limit)
    return pltpu.CompilerParams(vmem_limit_bytes=limit, collective_id=number, has_side_effects=True)


def shape(dims, kind):
    return jax.ShapeDtypeStruct(dims, kind)


def sems(count):
    return [pltpu.SemaphoreType.DMA((count,)), pltpu.SemaphoreType.DMA((count,)), pltpu.SemaphoreType.DMA((4,))]


def body(
    features, input_weight, output_weight, cotangent, adjacency_tiles, block_columns, graph_sizes
):
    row = lax.axis_index("row")
    rows, reps = lax.axis_size("row"), lax.axis_size("rep")
    blocks, per, tile = adjacency_tiles.shape[:3]
    local = blocks * tile
    fin = features.shape[1]
    hid = output_weight.shape[0]
    half, quarter = hid // reps, local // reps
    nodes = rows * local
    ends = jnp.cumsum(graph_sizes)

    def graph_of(places):
        return jnp.sum((places[..., None] >= ends).astype(jnp.int32), axis=-1)

    spots = lax.rem((row - HOPS) * local + nodes + jnp.arange(SPAN * local, dtype=jnp.int32), nodes)
    ids = graph_of(spots)
    row_ids = ids[HOPS * local:(HOPS + 1) * local].reshape(local, 1)
    band_ids = ids.reshape(SPAN * blocks, tile)
    padded = jnp.pad(block_columns, ((0, 8 - blocks), (0, 128 - per)))
    band, cots, all_tiles, all_cols = pl.pallas_call(
        functools.partial(open_kernel, rows, reps),
        out_shape=(
            shape((SPAN, local, fin), BF16),
            shape((reps, quarter, hid), BF16),
            shape((reps,) + adjacency_tiles.shape, BF16),
            shape((reps, 8, 128), jnp.int32),
        ),
        in_specs=[ANY] * 4,
        out_specs=(ANY,) * 4,
        scratch_shapes=sems(3 * (reps - 1) + 2 * HOPS),
        compiler_params=params(0),
    )(features, cotangent, adjacency_tiles, padded)
    dense, first, preact, hidden, scaled, terms, own, degree = pl.pallas_call(
        functools.partial(front_kernel, rows, reps, blocks, tile),
        out_shape=(
            shape((local, SPAN * local), BF16),
            shape((local, fin), BF16),
            shape((local, half), F32),
            shape((local, half), BF16),
            shape((local, half), BF16),
            shape((SPAN, half, local), BF16),
            shape((local, half), F32),
            shape((local, 1), F32),
        ),
        in_specs=[VMEM, SMEM] + [VMEM] * 6,
        out_specs=(VMEM,) * 8,
        compiler_params=params(),
    )(all_tiles, all_cols, row_ids, band_ids, band, cots, input_weight, output_weight)
    hid_band, term_band = pl.pallas_call(
        functools.partial(band_kernel, rows),
        out_shape=(shape((SPAN, local, half), BF16), shape((SPAN - 1, half, local), BF16)),
        in_specs=[ANY] * 2,
        out_specs=(ANY,) * 2,
        scratch_shapes=sems(4 * HOPS),
        compiler_params=params(1),
    )(hidden, terms)
    tall = hid * hid // reps // half + fin
    second, grads = pl.pallas_call(
        back_kernel,
        out_shape=(shape((local, half), BF16), shape((tall, half), F32)),
        in_specs=[VMEM] * 8,
        out_specs=(VMEM,) * 2,
        compiler_params=params(),
    )(dense, hid_band, term_band, first, preact, own, degree, cots)
    second = second.reshape(reps, quarter, half)
    if rows <= 16 and rows % 2 == 0 and tall % (8 * rows) == 0:
        chips = rows // 2
        chunk = tall // rows
        full, whole = pl.pallas_call(
            functools.partial(sum_kernel, chips, reps),
            out_shape=(shape((reps, quarter, half), BF16), shape((reps, 2, chips, chunk, half), F32)),
            in_specs=[ANY, VMEM],
            out_specs=(ANY, VMEM),
            scratch_shapes=[
                pltpu.VMEM((chips, chunk, half), F32),
                pltpu.VMEM((chips, chunk, half), F32),
                pltpu.VMEM((chips - 1, chunk, half), F32),
            ] + sems(3 * reps + 2 * chips),
            compiler_params=params(2),
        )(second, grads.reshape(2, chips, chunk, half))
        whole = whole.reshape(reps, tall, half)
    else:
        full = pl.pallas_call(
            functools.partial(swap_kernel, reps),
            out_shape=shape((reps, quarter, half), BF16),
            in_specs=[ANY],
            out_specs=ANY,
            scratch_shapes=sems(reps),
            compiler_params=params(2),
        )(second)
        whole = lax.all_gather(lax.psum(grads, "row"), "rep", axis=0)
    scores = dot(full.transpose(1, 0, 2).reshape(quarter, hid), output_weight, (1, 0)).astype(BF16)
    grad_input = whole[:, tall - fin:].transpose(1, 0, 2).reshape(fin, hid)
    grad_output = whole[:, :tall - fin].reshape(reps, hid // half, half, half)
    grad_output = grad_output.transpose(0, 2, 1, 3).reshape(hid, hid)
    return scores, grad_input, grad_output


def solution(mesh):
    placed = (
        P("row", None),
        P(),
        P(),
        P(("row", "rep"), None),
        P("row", "rep", None, None),
        P("row", "rep"),
        P(),
    )
    return jax.shard_map(
        body,
        mesh=mesh,
        in_specs=placed,
        out_specs=(P(("row", "rep"), None), P(), P()),
        check_vma=False,
    )
```

```python
import functools

import jax
import jax.numpy as jnp
from jax import lax
from jax.experimental import pallas as pl
from jax.experimental.pallas import tpu as pltpu
from jax.sharding import PartitionSpec as P

HOPS = 3
SPAN = 2 * HOPS + 1
MESH = pl.DeviceIdType.MESH
ANY = pl.BlockSpec(memory_space=pl.ANY)
HBM = pl.BlockSpec(memory_space=pltpu.HBM)
VMEM = pl.BlockSpec(memory_space=pltpu.VMEM)
SMEM = pl.BlockSpec(memory_space=pltpu.SMEM)
F32 = jnp.float32
BF16 = jnp.bfloat16


def dot(a, b, dims):
    return lax.dot_general(a, b, ((dims[:1], dims[1:]), ((), ())), preferred_element_type=F32)


def greet(peers):
    barrier = pltpu.get_barrier_semaphore()
    for peer in peers:
        pl.semaphore_signal(barrier, inc=1, device_id=peer, device_id_type=MESH)
    pl.semaphore_wait(barrier, len(peers))


def remote(src, dst, send, recv, index, peer):
    return pltpu.make_async_remote_copy(
        src_ref=src, dst_ref=dst, send_sem=send.at[index], recv_sem=recv.at[index],
        device_id=peer, device_id_type=MESH,
    )


def places(rows):
    row, rep = lax.axis_index("row"), lax.axis_index("rep")
    core = lax.rem(row, 2)
    flip, far = 1 - 2 * core, 6 * core - 3

    def at(shift):
        return (lax.rem(row + shift + rows, rows), rep)

    return flip, far, at


def start_rows(rows, src, band, send, recv, base):
    flip, far, at = places(rows)
    copies = [remote(src, band.at[HOPS - shift], send, recv, base + n, at(shift))
              for n, shift in enumerate((2, -2, far, flip))]
    for copy in copies:
        copy.start()
    return copies


def finish_rows(rows, copies, band, send, recv, base):
    flip, far, at = places(rows)
    passed = []
    for n, shift in enumerate((2, -2)):
        copies[n].wait_recv()
        step = remote(band.at[HOPS - shift], band.at[HOPS - shift - flip], send, recv, base + n, at(flip))
        step.start()
        passed.append(step)
    for copy in copies[2:]:
        copy.wait_recv()
    for copy in copies:
        copy.wait_send()
    for copy in passed:
        copy.wait()


def open_kernel(rows, reps, feats, cot, tiles, cols, band, cots, all_tiles, all_cols, send, recv, local):
    row, rep = lax.axis_index("row"), lax.axis_index("rep")
    flip, far, at = places(rows)
    others = [(row, lax.rem(rep + t, reps)) for t in range(1, reps)]
    greet([at(2), at(-2), at(far), at(flip)] + others)
    copies, n = [], 0
    pieces = ((tiles, all_tiles), (cols, all_cols), (cot, cots))
    for peer in others:
        for src, dst in pieces:
            copies.append(remote(src, dst.at[rep], send, recv, n, peer))
            n += 1
    for i, (src, dst) in enumerate(pieces):
        copies.append(pltpu.make_async_copy(src, dst.at[rep], local.at[i]))
    copies.append(pltpu.make_async_copy(feats, band.at[HOPS], local.at[3]))
    for copy in copies:
        copy.start()
    moved = start_rows(rows, feats, band, send, recv, n)
    finish_rows(rows, moved, band, send, recv, n + 4)
    for copy in copies:
        copy.wait()


def front_kernel(rows, reps, blocks, tile, tiles, cols, row_ids, band_ids, band, cots, w2,
                 dense, first_o, terms_o, own_o, deg_o):
    row, rep = lax.axis_index("row"), lax.axis_index("rep")
    total = rows * blocks
    per = tiles.shape[2]
    dense[...] = jnp.zeros_like(dense)
    for b in range(blocks):
        at = pl.ds(b * tile, tile)
        ids = row_ids[at, :]
        sums = jnp.ones((tile, 1), F32)
        for j in range(reps):
            for k in range(per):
                slot = lax.rem(cols[j, b, k] + total - (row - HOPS) * blocks, total)
                same = ids == band_ids[pl.ds(slot, 1), :]
                value = jnp.where(same, tiles[j, b, k].astype(F32), 0.0)
                sums = sums + jnp.sum(value, axis=1, keepdims=True)
                dense[at, pl.ds(pl.multiple_of(slot * tile, tile), tile)] = value.astype(BF16)
        deg_o[at, :] = sums
    degree = deg_o[...]
    local = blocks * tile
    flat = band[...].reshape(SPAN * local, -1)
    summed = dot(dense[...], flat, (1, 0))
    first = ((summed + band[HOPS].astype(F32)) / degree).astype(BF16)
    first_o[...] = first
    half = w2.shape[0] // reps
    at = pl.ds(pl.multiple_of(rep * half, half), half)
    pulled = dot(cots[...].reshape(local, -1), w2[at, :], (1, 1))
    scaled = (pulled / degree).astype(BF16)
    scaled_t = scaled.astype(F32).T.astype(BF16)
    for s in range(SPAN):
        part = dot(scaled_t, dense[:, s * local:(s + 1) * local], (1, 0))
        if s == HOPS:
            own_o[...] = part.T + scaled.astype(F32)
        terms_o[s] = part.astype(BF16)


def band_kernel(rows, first, terms, first_band, term_band, pair, joint, send, recv, local):
    flip, far, at = places(rows)
    greet([at(2), at(-2), at(far), at(flip)])
    joined = [remote(terms.at[HOPS + shift + flip], pair.at[n], send, recv, n, at(flip))
              for n, shift in enumerate((2, -2))]
    for copy in joined:
        copy.start()
    direct = [remote(terms.at[HOPS + far], term_band.at[2], send, recv, 2, at(far))]
    direct[0].start()
    moved = start_rows(rows, first, first_band, send, recv, 3)
    keep = pltpu.make_async_copy(first, first_band.at[HOPS], local.at[0])
    keep.start()
    direct.append(remote(terms.at[HOPS + flip], term_band.at[3], send, recv, 7, at(flip)))
    direct[1].start()
    for n, shift in enumerate((2, -2)):
        joined[n].wait_recv()
        joint[n] = (terms[HOPS + shift].astype(F32) + pair[n].astype(F32)).astype(BF16)
        step = remote(joint.at[n], term_band.at[n], send, recv, 8 + n, at(shift))
        step.start()
        direct.append(step)
    finish_rows(rows, moved, first_band, send, recv, 10)
    keep.wait()
    for copy in joined:
        copy.wait_send()
    for copy in direct:
        copy.wait()


def back_kernel(reps, dense, first_band, term_band, w1, own, deg, cots, second_o, grads_o):
    rep = lax.axis_index("rep")
    local, half = own.shape
    weight = w1[:, pl.ds(pl.multiple_of(rep * half, half), half)]
    preact = dot(first_band[HOPS], weight, (1, 0))
    mine = jnp.maximum(preact, 0.0).astype(BF16)
    summed = mine.astype(F32)
    for s in range(SPAN):
        hidden = mine if s == HOPS else jnp.maximum(dot(first_band[s], weight, (1, 0)), 0.0).astype(BF16)
        summed = summed + dot(dense[:, s * local:(s + 1) * local], hidden, (1, 0))
    second = (summed / deg[...]).astype(BF16)
    second_o[...] = second
    out = dot(second, cots[...].reshape(local, -1), (0, 0))
    width = out.shape[1] // half
    for i in range(width):
        grads_o[i * half:(i + 1) * half, :] = out[:, i * half:(i + 1) * half]
    got = term_band[0].astype(F32)
    for i in range(1, 4):
        got = got + term_band[i].astype(F32)
    back = got.T + own[...]
    delta = jnp.where(preact > 0.0, back, 0.0).astype(BF16)
    grads_o[width * half:, :] = dot(first_band[HOPS], delta, (0, 0))


def swap_kernel(reps, second, full, send, recv, local):
    row, rep = lax.axis_index("row"), lax.axis_index("rep")
    others = [(row, lax.rem(rep + t, reps)) for t in range(1, reps)]
    greet(others)
    copies = [remote(second.at[peer[1]], full.at[rep], send, recv, n, peer) for n, peer in enumerate(others)]
    copies.append(pltpu.make_async_copy(second.at[rep], full.at[rep], local.at[0]))
    for copy in copies:
        copy.start()
    for copy in copies:
        copy.wait()


def sum_kernel(chips, reps, second, grads, full, whole, mine, pair, parts, send, recv, local):
    row, rep = lax.axis_index("row"), lax.axis_index("rep")
    chip, core = row // 2, lax.rem(row, 2)
    sibling = (chip * 2 + 1 - core, rep)
    turns = [lax.rem(chip + t, chips) for t in range(1, chips)]
    peers = [(q * 2 + core, rep) for q in turns]
    others = [(row, lax.rem(rep + t, reps)) for t in range(1, reps)]
    greet([sibling] + peers + others)
    a = remote(grads.at[1 - core], pair, send, recv, 0, sibling)
    a.start()
    early = [remote(second.at[peer[1]], full.at[rep], send, recv, 1 + n, peer) for n, peer in enumerate(others)]
    early.append(pltpu.make_async_copy(second.at[rep], full.at[rep], local.at[0]))
    for copy in early:
        copy.start()
    base = reps
    a.wait()
    mine[...] = grads[core] + pair[...]
    copies = [remote(mine.at[q], parts.at[t], send, recv, base + t, peer)
              for t, (q, peer) in enumerate(zip(turns, peers))]
    for copy in copies:
        copy.start()
    total = mine[chip]
    for t, copy in enumerate(copies):
        copy.wait_recv()
        total = total + parts[t]
    whole[rep, core, chip] = total.astype(BF16)
    base = base + chips - 1
    spread = [remote(whole.at[rep, core, chip], whole.at[rep, core, chip], send, recv, base + t, peer)
              for t, peer in enumerate(peers)]
    for copy in spread:
        copy.start()
    for copy in copies:
        copy.wait_send()
    for copy in spread:
        copy.wait()
    base = base + chips - 1
    block = whole.at[rep, core]
    last = [remote(block, block, send, recv, base + n, peer) for n, peer in enumerate(others)]
    base = base + reps - 1
    side = [remote(block, block, send, recv, base, sibling)]
    for copy in last + side:
        copy.start()
    for n, copy in enumerate(last):
        copy.wait_recv()
        came = whole.at[lax.rem(rep + reps - 1 - n, reps), core]
        step = remote(came, came, send, recv, base + 1 + n, sibling)
        step.start()
        side.append(step)
    for copy in last:
        copy.wait_send()
    for copy in side + early:
        copy.wait()


def params(number=None):
    limit = 48 << 20
    if number is None:
        return pltpu.CompilerParams(vmem_limit_bytes=limit)
    return pltpu.CompilerParams(vmem_limit_bytes=limit, collective_id=number, has_side_effects=True)


def shape(dims, kind):
    return jax.ShapeDtypeStruct(dims, kind)


def sems(count):
    return [pltpu.SemaphoreType.DMA((count,)), pltpu.SemaphoreType.DMA((count,)), pltpu.SemaphoreType.DMA((4,))]


def body(
    features, input_weight, output_weight, cotangent, adjacency_tiles, block_columns, graph_sizes
):
    row = lax.axis_index("row")
    rows, reps = lax.axis_size("row"), lax.axis_size("rep")
    blocks, per, tile = adjacency_tiles.shape[:3]
    local = blocks * tile
    fin = features.shape[1]
    hid = output_weight.shape[0]
    half, quarter = hid // reps, local // reps
    nodes = rows * local
    ends = jnp.cumsum(graph_sizes)

    def graph_of(places):
        return jnp.sum((places[..., None] >= ends).astype(jnp.int32), axis=-1)

    spots = lax.rem((row - HOPS) * local + nodes + jnp.arange(SPAN * local, dtype=jnp.int32), nodes)
    ids = graph_of(spots)
    row_ids = ids[HOPS * local:(HOPS + 1) * local].reshape(local, 1)
    band_ids = ids.reshape(SPAN * blocks, tile)
    padded = jnp.pad(block_columns, ((0, 8 - blocks), (0, 128 - per)))
    band, cots, all_tiles, all_cols = pl.pallas_call(
        functools.partial(open_kernel, rows, reps),
        out_shape=(
            shape((SPAN, local, fin), BF16),
            shape((reps, quarter, hid), BF16),
            shape((reps,) + adjacency_tiles.shape, BF16),
            shape((reps, 8, 128), jnp.int32),
        ),
        in_specs=[HBM] * 4,
        out_specs=(ANY,) * 4,
        scratch_shapes=sems(3 * (reps - 1) + 6),
        compiler_params=params(0),
    )(features, cotangent, adjacency_tiles, padded)
    dense, first, terms, own, degree = pl.pallas_call(
        functools.partial(front_kernel, rows, reps, blocks, tile),
        out_shape=(
            shape((local, SPAN * local), BF16),
            shape((local, fin), BF16),
            shape((SPAN, half, local), BF16),
            shape((local, half), F32),
            shape((local, 1), F32),
        ),
        in_specs=[VMEM, SMEM] + [VMEM] * 5,
        out_specs=(VMEM,) * 5,
        compiler_params=params(),
    )(all_tiles, all_cols, row_ids, band_ids, band, cots, output_weight)
    first_band, term_band = pl.pallas_call(
        functools.partial(band_kernel, rows),
        out_shape=(shape((SPAN, local, fin), BF16), shape((4, half, local), BF16)),
        in_specs=[VMEM] * 2,
        out_specs=(VMEM,) * 2,
        scratch_shapes=[pltpu.VMEM((2, half, local), BF16)] * 2 + sems(12),
        compiler_params=params(1),
    )(first, terms)
    tall = hid * hid // reps // half + fin
    second, grads = pl.pallas_call(
        functools.partial(back_kernel, reps),
        out_shape=(shape((local, half), BF16), shape((tall, half), F32)),
        in_specs=[VMEM] * 7,
        out_specs=(VMEM,) * 2,
        compiler_params=params(),
    )(dense, first_band, term_band, input_weight, own, degree, cots)
    second = second.reshape(reps, quarter, half)
    if rows <= 16 and rows % 2 == 0 and tall % (8 * rows) == 0:
        chips = rows // 2
        chunk = tall // rows
        full, whole = pl.pallas_call(
            functools.partial(sum_kernel, chips, reps),
            out_shape=(shape((reps, quarter, half), BF16), shape((reps, 2, chips, chunk, half), BF16)),
            in_specs=[ANY, VMEM],
            out_specs=(ANY, VMEM),
            scratch_shapes=[
                pltpu.VMEM((chips, chunk, half), F32),
                pltpu.VMEM((chips, chunk, half), F32),
                pltpu.VMEM((chips - 1, chunk, half), F32),
            ] + sems(3 * reps + 2 * chips),
            compiler_params=params(2),
        )(second, grads.reshape(2, chips, chunk, half))
        whole = whole.reshape(reps, tall, half)
    else:
        full = pl.pallas_call(
            functools.partial(swap_kernel, reps),
            out_shape=shape((reps, quarter, half), BF16),
            in_specs=[ANY],
            out_specs=ANY,
            scratch_shapes=sems(reps),
            compiler_params=params(2),
        )(second)
        whole = lax.all_gather(lax.psum(grads, "row"), "rep", axis=0)
    scores = dot(full.transpose(1, 0, 2).reshape(quarter, hid), output_weight, (1, 0)).astype(BF16)
    whole = whole.astype(F32)
    grad_input = whole[:, tall - fin:].transpose(1, 0, 2).reshape(fin, hid)
    grad_output = whole[:, :tall - fin].reshape(reps, hid // half, half, half)
    grad_output = grad_output.transpose(0, 2, 1, 3).reshape(hid, hid)
    return scores, grad_input, grad_output


def solution(mesh):
    placed = (
        P("row", None),
        P(),
        P(),
        P(("row", "rep"), None),
        P("row", "rep", None, None),
        P("row", "rep"),
        P(),
    )
    return jax.shard_map(
        body,
        mesh=mesh,
        in_specs=placed,
        out_specs=(P(("row", "rep"), None), P(), P()),
        check_vma=False,
    )
```

```python
import functools

import jax
import jax.numpy as jnp
from jax import lax
from jax.experimental import pallas as pl
from jax.experimental.pallas import tpu as pltpu
from jax.sharding import PartitionSpec as P

HOPS = 3
SPAN = 2 * HOPS + 1
MESH = pl.DeviceIdType.MESH
ANY = pl.BlockSpec(memory_space=pl.ANY)
HBM = pl.BlockSpec(memory_space=pltpu.HBM)
VMEM = pl.BlockSpec(memory_space=pltpu.VMEM)
SMEM = pl.BlockSpec(memory_space=pltpu.SMEM)
F32 = jnp.float32
BF16 = jnp.bfloat16


def dot(a, b, dims):
    return lax.dot_general(a, b, ((dims[:1], dims[1:]), ((), ())), preferred_element_type=F32)


def greet(peers):
    barrier = pltpu.get_barrier_semaphore()
    for peer in peers:
        pl.semaphore_signal(barrier, inc=1, device_id=peer, device_id_type=MESH)
    pl.semaphore_wait(barrier, len(peers))


def remote(src, dst, send, recv, index, peer):
    return pltpu.make_async_remote_copy(
        src_ref=src, dst_ref=dst, send_sem=send.at[index], recv_sem=recv.at[index],
        device_id=peer, device_id_type=MESH,
    )


def places(rows):
    row, rep = lax.axis_index("row"), lax.axis_index("rep")
    core = lax.rem(row, 2)
    flip, far = 1 - 2 * core, 6 * core - 3

    def at(shift):
        return (lax.rem(row + shift + rows, rows), rep)

    return flip, far, at


def start_rows(rows, src, band, send, recv, base):
    flip, far, at = places(rows)
    copies = [remote(src, band.at[HOPS - shift], send, recv, base + n, at(shift))
              for n, shift in enumerate((2, -2, far, flip))]
    for copy in copies:
        copy.start()
    return copies


def finish_rows(rows, copies, band, send, recv, base):
    flip, far, at = places(rows)
    passed = []
    for n, shift in enumerate((2, -2)):
        copies[n].wait_recv()
        step = remote(band.at[HOPS - shift], band.at[HOPS - shift - flip], send, recv, base + n, at(flip))
        step.start()
        passed.append(step)
    for copy in copies[2:]:
        copy.wait_recv()
    for copy in copies:
        copy.wait_send()
    for copy in passed:
        copy.wait()


def open_kernel(rows, reps, feats, cot, tiles, cols, band, cots, all_tiles, all_cols, send, recv, local):
    row, rep = lax.axis_index("row"), lax.axis_index("rep")
    flip, far, at = places(rows)
    others = [(row, lax.rem(rep + t, reps)) for t in range(1, reps)]
    greet([at(2), at(-2), at(far), at(flip)] + others)
    copies, n = [], 0
    pieces = ((tiles, all_tiles), (cols, all_cols), (cot, cots))
    for peer in others:
        for src, dst in pieces:
            copies.append(remote(src, dst.at[rep], send, recv, n, peer))
            n += 1
    for i, (src, dst) in enumerate(pieces):
        copies.append(pltpu.make_async_copy(src, dst.at[rep], local.at[i]))
    copies.append(pltpu.make_async_copy(feats, band.at[HOPS], local.at[3]))
    for copy in copies:
        copy.start()
    moved = start_rows(rows, feats, band, send, recv, n)
    finish_rows(rows, moved, band, send, recv, n + 4)
    for copy in copies:
        copy.wait()


def front_kernel(rows, reps, blocks, tile, tiles, cols, row_ids, band_ids, band, cots, w2,
                 dense, first_o, terms_o, own_o, deg_o):
    row, rep = lax.axis_index("row"), lax.axis_index("rep")
    total = rows * blocks
    per = tiles.shape[2]
    dense[...] = jnp.zeros_like(dense)
    for b in range(blocks):
        at = pl.ds(b * tile, tile)
        ids = row_ids[at, :]
        sums = jnp.ones((tile, 1), F32)
        for j in range(reps):
            for k in range(per):
                slot = lax.rem(cols[j, b, k] + total - (row - HOPS) * blocks, total)
                same = ids == band_ids[pl.ds(slot, 1), :]
                value = jnp.where(same, tiles[j, b, k].astype(F32), 0.0)
                sums = sums + jnp.sum(value, axis=1, keepdims=True)
                dense[at, pl.ds(pl.multiple_of(slot * tile, tile), tile)] = value.astype(BF16)
        deg_o[at, :] = sums
    degree = deg_o[...]
    local = blocks * tile
    flat = band[...].reshape(SPAN * local, -1)
    summed = dot(dense[...], flat, (1, 0))
    first = ((summed + band[HOPS].astype(F32)) / degree).astype(BF16)
    first_o[...] = first
    half = w2.shape[0] // reps
    at = pl.ds(pl.multiple_of(rep * half, half), half)
    pulled = dot(cots[...].reshape(local, -1), w2[at, :], (1, 1))
    scaled = (pulled / degree).astype(BF16)
    scaled_t = scaled.astype(F32).T.astype(BF16)
    for s in range(SPAN):
        part = dot(scaled_t, dense[:, s * local:(s + 1) * local], (1, 0))
        if s == HOPS:
            own_o[...] = part.T + scaled.astype(F32)
        terms_o[s] = part.astype(BF16)


def band_kernel(rows, first, terms, first_band, term_band, pair, joint, send, recv, local):
    flip, far, at = places(rows)
    greet([at(2), at(-2), at(far), at(flip)])
    joined = [remote(terms.at[HOPS + shift + flip], pair.at[n], send, recv, n, at(flip))
              for n, shift in enumerate((2, -2))]
    for copy in joined:
        copy.start()
    direct = [remote(terms.at[HOPS + far], term_band.at[2], send, recv, 2, at(far))]
    direct[0].start()
    moved = start_rows(rows, first, first_band, send, recv, 3)
    keep = pltpu.make_async_copy(first, first_band.at[HOPS], local.at[0])
    keep.start()
    direct.append(remote(terms.at[HOPS + flip], term_band.at[3], send, recv, 7, at(flip)))
    direct[1].start()
    for n, shift in enumerate((2, -2)):
        joined[n].wait_recv()
        joint[n] = (terms[HOPS + shift].astype(F32) + pair[n].astype(F32)).astype(BF16)
        step = remote(joint.at[n], term_band.at[n], send, recv, 8 + n, at(shift))
        step.start()
        direct.append(step)
    finish_rows(rows, moved, first_band, send, recv, 10)
    keep.wait()
    for copy in joined:
        copy.wait_send()
    for copy in direct:
        copy.wait()


def back_kernel(reps, dense, first_band, term_band, w1, own, deg, cots, second_o, grads_o):
    rep = lax.axis_index("rep")
    local, half = own.shape
    weight = w1[:, pl.ds(pl.multiple_of(rep * half, half), half)]
    preact = dot(first_band[HOPS], weight, (1, 0))
    mine = jnp.maximum(preact, 0.0).astype(BF16)
    summed = mine.astype(F32)
    for s in range(SPAN):
        hidden = mine if s == HOPS else jnp.maximum(dot(first_band[s], weight, (1, 0)), 0.0).astype(BF16)
        summed = summed + dot(dense[:, s * local:(s + 1) * local], hidden, (1, 0))
    second = (summed / deg[...]).astype(BF16)
    second_o[...] = second
    out = dot(second, cots[...].reshape(local, -1), (0, 0))
    width = out.shape[1] // half
    for i in range(width):
        grads_o[i * half:(i + 1) * half, :] = out[:, i * half:(i + 1) * half]
    got = term_band[0].astype(F32)
    for i in range(1, 4):
        got = got + term_band[i].astype(F32)
    back = got.T + own[...]
    delta = jnp.where(preact > 0.0, back, 0.0).astype(BF16)
    grads_o[width * half:, :] = dot(first_band[HOPS], delta, (0, 0))


def swap_kernel(reps, second, full, send, recv, local):
    row, rep = lax.axis_index("row"), lax.axis_index("rep")
    others = [(row, lax.rem(rep + t, reps)) for t in range(1, reps)]
    greet(others)
    copies = [remote(second.at[peer[1]], full.at[rep], send, recv, n, peer) for n, peer in enumerate(others)]
    copies.append(pltpu.make_async_copy(second.at[rep], full.at[rep], local.at[0]))
    for copy in copies:
        copy.start()
    for copy in copies:
        copy.wait()


def rest_kernel(rows, reps, first, terms, dense, w1, own, deg, cots, full, whole,
                first_band, term_band, pair, joint, second_s, go, gi, go_pair, gi_pair, go_mine, gi_mine,
                go_parts, gi_parts, send, recv, local):
    row, rep = lax.axis_index("row"), lax.axis_index("rep")
    flip, far, at = places(rows)
    chips = rows // 2
    chip, core = row // 2, lax.rem(row, 2)
    sibling = at(flip)
    turns = [lax.rem(chip + t, chips) for t in range(1, chips)]
    peers = [(q * 2 + core, rep) for q in turns]
    others = [(row, lax.rem(rep + t, reps)) for t in range(1, reps)]
    greet([sibling, at(far)] + peers + others)
    joined = [remote(terms.at[HOPS + shift + flip], pair.at[n], send, recv, n, sibling)
              for n, shift in enumerate((2, -2))]
    for copy in joined:
        copy.start()
    moved = start_rows(rows, first, first_band, send, recv, 3)
    direct = [remote(terms.at[HOPS + far], term_band.at[2], send, recv, 2, at(far))]
    direct[0].start()
    keep = pltpu.make_async_copy(first, first_band.at[HOPS], local.at[0])
    keep.start()
    direct.append(remote(terms.at[HOPS + flip], term_band.at[3], send, recv, 7, sibling))
    direct[1].start()
    for n, shift in enumerate((2, -2)):
        joined[n].wait_recv()
        joint[n] = (terms[HOPS + shift].astype(F32) + pair[n].astype(F32)).astype(BF16)
        step = remote(joint.at[n], term_band.at[n], send, recv, 8 + n, at(shift))
        step.start()
        direct.append(step)
    finish_rows(rows, moved, first_band, send, recv, 10)
    keep.wait()

    size, half = own.shape
    weight = w1[:, pl.ds(pl.multiple_of(rep * half, half), half)]
    mine_first = first_band[HOPS]
    preact = dot(mine_first, weight, (1, 0))
    mine = jnp.maximum(preact, 0.0).astype(BF16)
    summed = mine.astype(F32)
    for s in range(SPAN):
        hidden = mine if s == HOPS else jnp.maximum(dot(first_band[s], weight, (1, 0)), 0.0).astype(BF16)
        summed = summed + dot(dense[:, s * size:(s + 1) * size], hidden, (1, 0))
    second = (summed / deg[...]).astype(BF16)
    second_s[...] = second.reshape(second_s.shape)
    base = 12
    late = [remote(second_s.at[peer[1]], full.at[rep], send, recv, base + n, peer) for n, peer in enumerate(others)]
    late.append(pltpu.make_async_copy(second_s.at[rep], full.at[rep], local.at[1]))
    for copy in late:
        copy.start()
    base = base + reps - 1
    out = dot(second, cots[...].reshape(size, -1), (0, 0))
    width = out.shape[1] // half
    out = jnp.concatenate([out[:, i * half:(i + 1) * half] for i in range(width)], axis=0)
    go[...] = out.reshape(go.shape)

    def fold(grads, got, total, parts, base):
        a = remote(grads.at[1 - core], got, send, recv, base, sibling)
        a.start()

        def rest():
            a.wait()
            total[...] = grads[core] + got[...]
            copies = [remote(total.at[q], parts.at[t], send, recv, base + 1 + t, peer)
                      for t, (q, peer) in enumerate(zip(turns, peers))]
            for copy in copies:
                copy.start()
            return copies

        return rest

    def gathered(copies, total, parts):
        value = total[chip]
        for t, copy in enumerate(copies):
            copy.wait_recv()
            value = value + parts[t]
        return value

    go_copies = fold(go, go_pair, go_mine, go_parts, base)()
    base = base + chips
    for copy in direct:
        copy.wait()
    got = term_band[0].astype(F32)
    for i in range(1, 4):
        got = got + term_band[i].astype(F32)
    back = got.T + own[...]
    delta = jnp.where(preact > 0.0, back, 0.0).astype(BF16)
    gi[...] = dot(mine_first, delta, (0, 0)).reshape(gi.shape)
    rest = fold(gi, gi_pair, gi_mine, gi_parts, base)
    base = base + chips
    go_total = gathered(go_copies, go_mine, go_parts)
    gi_copies = rest()
    gi_total = gathered(gi_copies, gi_mine, gi_parts)
    whole[rep, core, chip] = jnp.concatenate([go_total, gi_total], axis=0).astype(BF16)
    spot = whole.at[rep, core, chip]
    spread = [remote(spot, spot, send, recv, base + t, peer) for t, peer in enumerate(peers)]
    for copy in spread:
        copy.start()
    base = base + chips - 1
    for copy in joined + go_copies + gi_copies:
        copy.wait_send()
    for copy in spread:
        copy.wait()
    block = whole.at[rep, core]
    last = [remote(block, block, send, recv, base + n, peer) for n, peer in enumerate(others)]
    base = base + reps - 1
    side = [remote(block, block, send, recv, base, sibling)]
    for copy in last + side:
        copy.start()
    for n, copy in enumerate(last):
        copy.wait_recv()
        came = whole.at[lax.rem(rep + reps - 1 - n, reps), core]
        step = remote(came, came, send, recv, base + 1 + n, sibling)
        step.start()
        side.append(step)
    for copy in last:
        copy.wait_send()
    for copy in side + late:
        copy.wait()


def close_kernel(deep, full, whole, w2, scores_o, gi_o, go_o):
    reps, half = full.shape[0], full.shape[2]
    for j in range(reps):
        at = slice(j * half, (j + 1) * half)
        part = dot(full[j], w2[at, :], (1, 0))
        total = part if j == 0 else total + part
        part = whole[j].astype(F32)
        gi_o[:, at] = part[..., deep:, :].reshape(gi_o.shape[0], half)
        part = part[..., :deep, :].reshape(-1, half)
        for i in range(part.shape[0] // half):
            go_o[at, i * half:(i + 1) * half] = part[i * half:(i + 1) * half]
    scores_o[...] = total.astype(BF16)


def params(number=None):
    limit = 48 << 20
    if number is None:
        return pltpu.CompilerParams(vmem_limit_bytes=limit)
    return pltpu.CompilerParams(vmem_limit_bytes=limit, collective_id=number, has_side_effects=True)


def shape(dims, kind):
    return jax.ShapeDtypeStruct(dims, kind)


def sems(count):
    return [pltpu.SemaphoreType.DMA((count,)), pltpu.SemaphoreType.DMA((count,)), pltpu.SemaphoreType.DMA((4,))]


def body(
    features, input_weight, output_weight, cotangent, adjacency_tiles, block_columns, graph_sizes
):
    row = lax.axis_index("row")
    rows, reps = lax.axis_size("row"), lax.axis_size("rep")
    blocks, per, tile = adjacency_tiles.shape[:3]
    local = blocks * tile
    fin = features.shape[1]
    hid = output_weight.shape[0]
    half, quarter = hid // reps, local // reps
    nodes = rows * local
    ends = jnp.cumsum(graph_sizes)

    def graph_of(places):
        return jnp.sum((places[..., None] >= ends).astype(jnp.int32), axis=-1)

    spots = lax.rem((row - HOPS) * local + nodes + jnp.arange(SPAN * local, dtype=jnp.int32), nodes)
    ids = graph_of(spots)
    row_ids = ids[HOPS * local:(HOPS + 1) * local].reshape(local, 1)
    band_ids = ids.reshape(SPAN * blocks, tile)
    padded = jnp.pad(block_columns, ((0, 8 - blocks), (0, 128 - per)))
    band, cots, all_tiles, all_cols = pl.pallas_call(
        functools.partial(open_kernel, rows, reps),
        out_shape=(
            shape((SPAN, local, fin), BF16),
            shape((reps, quarter, hid), BF16),
            shape((reps,) + adjacency_tiles.shape, BF16),
            shape((reps, 8, 128), jnp.int32),
        ),
        in_specs=[HBM] * 4,
        out_specs=(VMEM,) * 3 + (ANY,),
        scratch_shapes=sems(3 * (reps - 1) + 6),
        compiler_params=params(0),
    )(features, cotangent, adjacency_tiles, padded)
    dense, first, terms, own, degree = pl.pallas_call(
        functools.partial(front_kernel, rows, reps, blocks, tile),
        out_shape=(
            shape((local, SPAN * local), BF16),
            shape((local, fin), BF16),
            shape((SPAN, half, local), BF16),
            shape((local, half), F32),
            shape((local, 1), F32),
        ),
        in_specs=[VMEM, SMEM] + [VMEM] * 5,
        out_specs=(VMEM,) * 5,
        compiler_params=params(),
    )(all_tiles, all_cols, row_ids, band_ids, band, cots, output_weight)
    tall = hid * hid // reps // half + fin
    if 6 < rows <= 16 and rows % 2 == 0 and fin % (8 * rows) == 0:
        chips, deep, thin = rows // 2, hid // rows, fin // rows

        def bank(*dims):
            return pltpu.VMEM(dims, F32)

        full, whole = pl.pallas_call(
            functools.partial(rest_kernel, rows, reps),
            out_shape=(
                shape((reps, quarter, half), BF16),
                shape((reps, 2, chips, deep + thin, half), BF16),
            ),
            in_specs=[VMEM] * 7,
            out_specs=(VMEM,) * 2,
            scratch_shapes=[
                pltpu.VMEM((SPAN, local, fin), BF16),
                pltpu.VMEM((4, half, local), BF16),
                pltpu.VMEM((2, half, local), BF16),
                pltpu.VMEM((2, half, local), BF16),
                pltpu.VMEM((reps, quarter, half), BF16),
                bank(2, chips, deep, half),
                bank(2, chips, thin, half),
                bank(chips, deep, half),
                bank(chips, thin, half),
                bank(chips, deep, half),
                bank(chips, thin, half),
                bank(chips - 1, deep, half),
                bank(chips - 1, thin, half),
            ] + sems(12 + 3 * reps + 3 * chips),
            compiler_params=params(1),
        )(first, terms, dense, input_weight, own, degree, cots)
        scores, grad_input, grad_output = pl.pallas_call(
            functools.partial(close_kernel, deep),
            out_shape=(shape((quarter, hid), BF16), shape((fin, hid), F32), shape((hid, hid), F32)),
            in_specs=[VMEM] * 3,
            out_specs=(VMEM,) * 3,
            compiler_params=params(),
        )(full, whole, output_weight)
        return scores, grad_input, grad_output
    first_band, term_band = pl.pallas_call(
        functools.partial(band_kernel, rows),
        out_shape=(shape((SPAN, local, fin), BF16), shape((4, half, local), BF16)),
        in_specs=[VMEM] * 2,
        out_specs=(VMEM,) * 2,
        scratch_shapes=[pltpu.VMEM((2, half, local), BF16)] * 2 + sems(12),
        compiler_params=params(1),
    )(first, terms)
    second, grads = pl.pallas_call(
        functools.partial(back_kernel, reps),
        out_shape=(shape((local, half), BF16), shape((tall, half), F32)),
        in_specs=[VMEM] * 7,
        out_specs=(VMEM,) * 2,
        compiler_params=params(),
    )(dense, first_band, term_band, input_weight, own, degree, cots)
    second = second.reshape(reps, quarter, half)
    full = pl.pallas_call(
        functools.partial(swap_kernel, reps),
        out_shape=shape((reps, quarter, half), BF16),
        in_specs=[ANY],
        out_specs=ANY,
        scratch_shapes=sems(reps),
        compiler_params=params(2),
    )(second)
    whole = lax.all_gather(lax.psum(grads, "row"), "rep", axis=0)
    scores = dot(full.transpose(1, 0, 2).reshape(quarter, hid), output_weight, (1, 0)).astype(BF16)
    grad_input = whole[:, tall - fin:].transpose(1, 0, 2).reshape(fin, hid)
    grad_output = whole[:, :tall - fin].reshape(reps, hid // half, half, half)
    grad_output = grad_output.transpose(0, 2, 1, 3).reshape(hid, hid)
    return scores, grad_input, grad_output


def solution(mesh):
    placed = (
        P("row", None),
        P(),
        P(),
        P(("row", "rep"), None),
        P("row", "rep", None, None),
        P("row", "rep"),
        P(),
    )
    return jax.shard_map(
        body,
        mesh=mesh,
        in_specs=placed,
        out_specs=(P(("row", "rep"), None), P(), P()),
        check_vma=False,
    )
```

```python
import functools

import jax
import jax.numpy as jnp
from jax import lax
from jax.experimental import pallas as pl
from jax.experimental.pallas import tpu as pltpu
from jax.sharding import PartitionSpec as P

HOPS = 3
SPAN = 2 * HOPS + 1
MESH = pl.DeviceIdType.MESH
ANY = pl.BlockSpec(memory_space=pl.ANY)
HBM = pl.BlockSpec(memory_space=pltpu.HBM)
VMEM = pl.BlockSpec(memory_space=pltpu.VMEM)
SMEM = pl.BlockSpec(memory_space=pltpu.SMEM)
F32 = jnp.float32
BF16 = jnp.bfloat16


def dot(a, b, dims):
    return lax.dot_general(a, b, ((dims[:1], dims[1:]), ((), ())), preferred_element_type=F32)


def greet(peers):
    barrier = pltpu.get_barrier_semaphore()
    for peer in peers:
        pl.semaphore_signal(barrier, inc=1, device_id=peer, device_id_type=MESH)
    pl.semaphore_wait(barrier, len(peers))


def remote(src, dst, send, recv, index, peer):
    return pltpu.make_async_remote_copy(
        src_ref=src, dst_ref=dst, send_sem=send.at[index], recv_sem=recv.at[index],
        device_id=peer, device_id_type=MESH,
    )


def places(rows):
    row, rep = lax.axis_index("row"), lax.axis_index("rep")
    core = lax.rem(row, 2)
    flip, far = 1 - 2 * core, 6 * core - 3

    def at(shift):
        return (lax.rem(row + shift + rows, rows), rep)

    return flip, far, at


def start_rows(rows, src, band, send, recv, base):
    flip, far, at = places(rows)
    copies = [remote(src, band.at[HOPS - shift], send, recv, base + n, at(shift))
              for n, shift in enumerate((2, -2, far, flip))]
    for copy in copies:
        copy.start()
    return copies


def finish_rows(rows, copies, band, send, recv, base):
    flip, far, at = places(rows)
    passed = []
    for n, shift in enumerate((2, -2)):
        copies[n].wait_recv()
        step = remote(band.at[HOPS - shift], band.at[HOPS - shift - flip], send, recv, base + n, at(flip))
        step.start()
        passed.append(step)
    for copy in copies[2:]:
        copy.wait_recv()
    for copy in copies:
        copy.wait_send()
    for copy in passed:
        copy.wait()


def open_kernel(rows, reps, feats, cot, tiles, cols, band, cots, all_tiles, all_cols, send, recv, local):
    row, rep = lax.axis_index("row"), lax.axis_index("rep")
    flip, far, at = places(rows)
    others = [(row, lax.rem(rep + t, reps)) for t in range(1, reps)]
    greet([at(2), at(-2), at(far), at(flip)] + others)
    copies, n = [], 0
    pieces = ((tiles, all_tiles), (cols, all_cols), (cot, cots))
    pieces = pieces if cot is not None else pieces[:2]
    for peer in others:
        for src, dst in pieces:
            copies.append(remote(src, dst.at[rep], send, recv, n, peer))
            n += 1
    for i, (src, dst) in enumerate(pieces):
        copies.append(pltpu.make_async_copy(src, dst.at[rep], local.at[i]))
    copies.append(pltpu.make_async_copy(feats, band.at[HOPS], local.at[3]))
    for copy in copies:
        copy.start()
    moved = start_rows(rows, feats, band, send, recv, n)
    finish_rows(rows, moved, band, send, recv, n + 4)
    for copy in copies:
        copy.wait()


def scale_terms(rep, reps, cots, w2, dense, degree, terms):
    size = degree.shape[0]
    half = w2.shape[0] // reps
    at = pl.ds(pl.multiple_of(rep * half, half), half)
    pulled = dot(cots[...].reshape(size, -1), w2[at, :], (1, 1))
    scaled = (pulled / degree).astype(BF16)
    scaled_t = scaled.astype(F32).T.astype(BF16)
    for s in range(SPAN):
        part = dot(scaled_t, dense[:, s * size:(s + 1) * size], (1, 0))
        if s == HOPS:
            own = part.T + scaled.astype(F32)
        terms[s] = part.astype(BF16)
    return own


def share_kernel(rows, reps, feats, tiles, cols, band, all_tiles, all_cols, send, recv, local):
    open_kernel(rows, reps, feats, None, tiles, cols, band, None, all_tiles, all_cols, send, recv, local)


def front_kernel(rows, reps, blocks, tile, tiles, cols, row_ids, band_ids, band,
                 dense, first_o, deg_o):
    row = lax.axis_index("row")
    total = rows * blocks
    per = tiles.shape[2]
    dense[...] = jnp.zeros_like(dense)
    for b in range(blocks):
        at = pl.ds(b * tile, tile)
        ids = row_ids[at, :]
        sums = jnp.ones((tile, 1), F32)
        for j in range(reps):
            for k in range(per):
                slot = lax.rem(cols[j, b, k] + total - (row - HOPS) * blocks, total)
                same = ids == band_ids[pl.ds(slot, 1), :]
                value = jnp.where(same, tiles[j, b, k].astype(F32), 0.0)
                sums = sums + jnp.sum(value, axis=1, keepdims=True)
                dense[at, pl.ds(pl.multiple_of(slot * tile, tile), tile)] = value.astype(BF16)
        deg_o[at, :] = sums
    degree = deg_o[...]
    local = blocks * tile
    flat = band[...].reshape(SPAN * local, -1)
    summed = dot(dense[...], flat, (1, 0))
    first = ((summed + band[HOPS].astype(F32)) / degree).astype(BF16)
    first_o[...] = first


def full_front_kernel(rows, reps, blocks, tile, tiles, cols, row_ids, band_ids, band, cots, w2,
                      dense, first_o, terms_o, own_o, deg_o):
    front_kernel(rows, reps, blocks, tile, tiles, cols, row_ids, band_ids, band, dense, first_o, deg_o)
    own_o[...] = scale_terms(lax.axis_index("rep"), reps, cots, w2, dense, deg_o[...], terms_o)


def band_kernel(rows, first, terms, first_band, term_band, pair, joint, send, recv, local):
    flip, far, at = places(rows)
    greet([at(2), at(-2), at(far), at(flip)])
    joined = [remote(terms.at[HOPS + shift + flip], pair.at[n], send, recv, n, at(flip))
              for n, shift in enumerate((2, -2))]
    for copy in joined:
        copy.start()
    direct = [remote(terms.at[HOPS + far], term_band.at[2], send, recv, 2, at(far))]
    direct[0].start()
    moved = start_rows(rows, first, first_band, send, recv, 3)
    keep = pltpu.make_async_copy(first, first_band.at[HOPS], local.at[0])
    keep.start()
    direct.append(remote(terms.at[HOPS + flip], term_band.at[3], send, recv, 7, at(flip)))
    direct[1].start()
    for n, shift in enumerate((2, -2)):
        joined[n].wait_recv()
        joint[n] = (terms[HOPS + shift].astype(F32) + pair[n].astype(F32)).astype(BF16)
        step = remote(joint.at[n], term_band.at[n], send, recv, 8 + n, at(shift))
        step.start()
        direct.append(step)
    finish_rows(rows, moved, first_band, send, recv, 10)
    keep.wait()
    for copy in joined:
        copy.wait_send()
    for copy in direct:
        copy.wait()


def back_kernel(reps, dense, first_band, term_band, w1, own, deg, cots, second_o, grads_o):
    rep = lax.axis_index("rep")
    local, half = own.shape
    weight = w1[:, pl.ds(pl.multiple_of(rep * half, half), half)]
    preact = dot(first_band[HOPS], weight, (1, 0))
    mine = jnp.maximum(preact, 0.0).astype(BF16)
    summed = mine.astype(F32)
    for s in range(SPAN):
        hidden = mine if s == HOPS else jnp.maximum(dot(first_band[s], weight, (1, 0)), 0.0).astype(BF16)
        summed = summed + dot(dense[:, s * local:(s + 1) * local], hidden, (1, 0))
    second = (summed / deg[...]).astype(BF16)
    second_o[...] = second
    out = dot(second, cots[...].reshape(local, -1), (0, 0))
    width = out.shape[1] // half
    for i in range(width):
        grads_o[i * half:(i + 1) * half, :] = out[:, i * half:(i + 1) * half]
    got = term_band[0].astype(F32)
    for i in range(1, 4):
        got = got + term_band[i].astype(F32)
    back = got.T + own[...]
    delta = jnp.where(preact > 0.0, back, 0.0).astype(BF16)
    grads_o[width * half:, :] = dot(first_band[HOPS], delta, (0, 0))


def swap_kernel(reps, second, full, send, recv, local):
    row, rep = lax.axis_index("row"), lax.axis_index("rep")
    others = [(row, lax.rem(rep + t, reps)) for t in range(1, reps)]
    greet(others)
    copies = [remote(second.at[peer[1]], full.at[rep], send, recv, n, peer) for n, peer in enumerate(others)]
    copies.append(pltpu.make_async_copy(second.at[rep], full.at[rep], local.at[0]))
    for copy in copies:
        copy.start()
    for copy in copies:
        copy.wait()


def rest_kernel(rows, reps, first, dense, w1, w2, deg, cot, full, whole,
                cots, terms, first_band, term_band, pair, joint, second_s, go, gi, go_pair, gi_pair, go_mine, gi_mine,
                go_parts, gi_parts, send, recv, local):
    row, rep = lax.axis_index("row"), lax.axis_index("rep")
    flip, far, at = places(rows)
    chips = rows // 2
    chip, core = row // 2, lax.rem(row, 2)
    sibling = at(flip)
    turns = [lax.rem(chip + t, chips) for t in range(1, chips)]
    peers = [(q * 2 + core, rep) for q in turns]
    others = [(row, lax.rem(rep + t, reps)) for t in range(1, reps)]
    greet([sibling, at(far)] + peers + others)
    swaps = [remote(cot, cots.at[rep], send, recv, 12 + n, peer) for n, peer in enumerate(others)]
    swaps.append(pltpu.make_async_copy(cot, cots.at[rep], local.at[2]))
    for copy in swaps:
        copy.start()
    moved = start_rows(rows, first, first_band, send, recv, 3)
    keep = pltpu.make_async_copy(first, first_band.at[HOPS], local.at[0])
    keep.start()
    for copy in swaps:
        copy.wait()
    own = scale_terms(rep, reps, cots, w2, dense, deg[...], terms)
    joined = [remote(terms.at[HOPS + shift + flip], pair.at[n], send, recv, n, sibling)
              for n, shift in enumerate((2, -2))]
    for copy in joined:
        copy.start()
    direct = [remote(terms.at[HOPS + far], term_band.at[2], send, recv, 2, at(far))]
    direct[0].start()
    direct.append(remote(terms.at[HOPS + flip], term_band.at[3], send, recv, 7, sibling))
    direct[1].start()
    for n, shift in enumerate((2, -2)):
        joined[n].wait_recv()
        joint[n] = (terms[HOPS + shift].astype(F32) + pair[n].astype(F32)).astype(BF16)
        step = remote(joint.at[n], term_band.at[n], send, recv, 8 + n, at(shift))
        step.start()
        direct.append(step)
    finish_rows(rows, moved, first_band, send, recv, 10)
    keep.wait()

    size, half = own.shape
    weight = w1[:, pl.ds(pl.multiple_of(rep * half, half), half)]
    mine_first = first_band[HOPS]
    preact = dot(mine_first, weight, (1, 0))
    mine = jnp.maximum(preact, 0.0).astype(BF16)
    summed = mine.astype(F32)
    for s in range(SPAN):
        hidden = mine if s == HOPS else jnp.maximum(dot(first_band[s], weight, (1, 0)), 0.0).astype(BF16)
        summed = summed + dot(dense[:, s * size:(s + 1) * size], hidden, (1, 0))
    second = (summed / deg[...]).astype(BF16)
    second_s[...] = second.reshape(second_s.shape)
    base = 11 + reps
    late = [remote(second_s.at[peer[1]], full.at[rep], send, recv, base + n, peer) for n, peer in enumerate(others)]
    late.append(pltpu.make_async_copy(second_s.at[rep], full.at[rep], local.at[1]))
    for copy in late:
        copy.start()
    base = base + reps - 1
    out = dot(second, cots[...].reshape(size, -1), (0, 0))
    width = out.shape[1] // half
    out = jnp.concatenate([out[:, i * half:(i + 1) * half] for i in range(width)], axis=0)
    go[...] = out.reshape(go.shape)

    def fold(grads, got, total, parts, base):
        a = remote(grads.at[1 - core], got, send, recv, base, sibling)
        a.start()

        def rest():
            a.wait()
            total[...] = grads[core] + got[...]
            copies = [remote(total.at[q], parts.at[t], send, recv, base + 1 + t, peer)
                      for t, (q, peer) in enumerate(zip(turns, peers))]
            for copy in copies:
                copy.start()
            return copies

        return rest

    def gathered(copies, total, parts):
        value = total[chip]
        for t, copy in enumerate(copies):
            copy.wait_recv()
            value = value + parts[t]
        return value

    go_copies = fold(go, go_pair, go_mine, go_parts, base)()
    base = base + chips
    for copy in direct:
        copy.wait()
    got = term_band[0].astype(F32)
    for i in range(1, 4):
        got = got + term_band[i].astype(F32)
    back = got.T + own
    delta = jnp.where(preact > 0.0, back, 0.0).astype(BF16)
    gi[...] = dot(mine_first, delta, (0, 0)).reshape(gi.shape)
    rest = fold(gi, gi_pair, gi_mine, gi_parts, base)
    base = base + chips
    go_total = gathered(go_copies, go_mine, go_parts)
    gi_copies = rest()
    gi_total = gathered(gi_copies, gi_mine, gi_parts)
    whole[rep, core, chip] = jnp.concatenate([go_total, gi_total], axis=0).astype(BF16)
    spot = whole.at[rep, core, chip]
    spread = [remote(spot, spot, send, recv, base + t, peer) for t, peer in enumerate(peers)]
    for copy in spread:
        copy.start()
    base = base + chips - 1
    for copy in joined + go_copies + gi_copies:
        copy.wait_send()
    for copy in spread:
        copy.wait()
    block = whole.at[rep, core]
    last = [remote(block, block, send, recv, base + n, peer) for n, peer in enumerate(others)]
    base = base + reps - 1
    side = [remote(block, block, send, recv, base, sibling)]
    for copy in last + side:
        copy.start()
    for n, copy in enumerate(last):
        copy.wait_recv()
        came = whole.at[lax.rem(rep + reps - 1 - n, reps), core]
        step = remote(came, came, send, recv, base + 1 + n, sibling)
        step.start()
        side.append(step)
    for copy in last:
        copy.wait_send()
    for copy in side + late:
        copy.wait()


def close_kernel(deep, full, whole, w2, scores_o, gi_o, go_o):
    reps, half = full.shape[0], full.shape[2]
    for j in range(reps):
        at = slice(j * half, (j + 1) * half)
        part = dot(full[j], w2[at, :], (1, 0))
        total = part if j == 0 else total + part
        part = whole[j].astype(F32)
        gi_o[:, at] = part[..., deep:, :].reshape(gi_o.shape[0], half)
        part = part[..., :deep, :].reshape(-1, half)
        for i in range(part.shape[0] // half):
            go_o[at, i * half:(i + 1) * half] = part[i * half:(i + 1) * half]
    scores_o[...] = total.astype(BF16)


def params(number=None):
    limit = 48 << 20
    if number is None:
        return pltpu.CompilerParams(vmem_limit_bytes=limit)
    return pltpu.CompilerParams(vmem_limit_bytes=limit, collective_id=number, has_side_effects=True)


def shape(dims, kind):
    return jax.ShapeDtypeStruct(dims, kind)


def sems(count):
    return [pltpu.SemaphoreType.DMA((count,)), pltpu.SemaphoreType.DMA((count,)), pltpu.SemaphoreType.DMA((4,))]


def body(
    features, input_weight, output_weight, cotangent, adjacency_tiles, block_columns, graph_sizes
):
    row = lax.axis_index("row")
    rows, reps = lax.axis_size("row"), lax.axis_size("rep")
    blocks, per, tile = adjacency_tiles.shape[:3]
    local = blocks * tile
    fin = features.shape[1]
    hid = output_weight.shape[0]
    half, quarter = hid // reps, local // reps
    nodes = rows * local
    ends = jnp.cumsum(graph_sizes)

    def graph_of(places):
        return jnp.sum((places[..., None] >= ends).astype(jnp.int32), axis=-1)

    spots = lax.rem((row - HOPS) * local + nodes + jnp.arange(SPAN * local, dtype=jnp.int32), nodes)
    ids = graph_of(spots)
    row_ids = ids[HOPS * local:(HOPS + 1) * local].reshape(local, 1)
    band_ids = ids.reshape(SPAN * blocks, tile)
    padded = jnp.pad(block_columns, ((0, 8 - blocks), (0, 128 - per)))
    tall = hid * hid // reps // half + fin
    if 6 < rows <= 16 and rows % 2 == 0 and fin % (8 * rows) == 0:
        chips, deep, thin = rows // 2, hid // rows, fin // rows

        band, all_tiles, all_cols = pl.pallas_call(
            functools.partial(share_kernel, rows, reps),
            out_shape=(
                shape((SPAN, local, fin), BF16),
                shape((reps,) + adjacency_tiles.shape, BF16),
                shape((reps, 8, 128), jnp.int32),
            ),
            in_specs=[HBM] * 3,
            out_specs=(VMEM,) * 2 + (ANY,),
            scratch_shapes=sems(2 * (reps - 1) + 6),
            compiler_params=params(0),
        )(features, adjacency_tiles, padded)
        dense, first, degree = pl.pallas_call(
            functools.partial(front_kernel, rows, reps, blocks, tile),
            out_shape=(
                shape((local, SPAN * local), BF16),
                shape((local, fin), BF16),
                shape((local, 1), F32),
            ),
            in_specs=[VMEM, SMEM] + [VMEM] * 3,
            out_specs=(VMEM,) * 3,
            compiler_params=params(),
        )(all_tiles, all_cols, row_ids, band_ids, band)

        def bank(*dims):
            return pltpu.VMEM(dims, F32)

        full, whole = pl.pallas_call(
            functools.partial(rest_kernel, rows, reps),
            out_shape=(
                shape((reps, quarter, half), BF16),
                shape((reps, 2, chips, deep + thin, half), BF16),
            ),
            in_specs=[VMEM] * 6,
            out_specs=(VMEM,) * 2,
            scratch_shapes=[
                pltpu.VMEM((reps, quarter, hid), BF16),
                pltpu.VMEM((SPAN, half, local), BF16),
                pltpu.VMEM((SPAN, local, fin), BF16),
                pltpu.VMEM((4, half, local), BF16),
                pltpu.VMEM((2, half, local), BF16),
                pltpu.VMEM((2, half, local), BF16),
                pltpu.VMEM((reps, quarter, half), BF16),
                bank(2, chips, deep, half),
                bank(2, chips, thin, half),
                bank(chips, deep, half),
                bank(chips, thin, half),
                bank(chips, deep, half),
                bank(chips, thin, half),
                bank(chips - 1, deep, half),
                bank(chips - 1, thin, half),
            ] + sems(12 + 4 * reps + 3 * chips),
            compiler_params=params(1),
        )(first, dense, input_weight, output_weight, degree, cotangent)
        scores, grad_input, grad_output = pl.pallas_call(
            functools.partial(close_kernel, deep),
            out_shape=(shape((quarter, hid), BF16), shape((fin, hid), F32), shape((hid, hid), F32)),
            in_specs=[VMEM] * 3,
            out_specs=(VMEM,) * 3,
            compiler_params=params(),
        )(full, whole, output_weight)
        return scores, grad_input, grad_output
    band, cots, all_tiles, all_cols = pl.pallas_call(
        functools.partial(open_kernel, rows, reps),
        out_shape=(
            shape((SPAN, local, fin), BF16),
            shape((reps, quarter, hid), BF16),
            shape((reps,) + adjacency_tiles.shape, BF16),
            shape((reps, 8, 128), jnp.int32),
        ),
        in_specs=[HBM] * 4,
        out_specs=(VMEM,) * 3 + (ANY,),
        scratch_shapes=sems(3 * (reps - 1) + 6),
        compiler_params=params(0),
    )(features, cotangent, adjacency_tiles, padded)
    dense, first, terms, own, degree = pl.pallas_call(
        functools.partial(full_front_kernel, rows, reps, blocks, tile),
        out_shape=(
            shape((local, SPAN * local), BF16),
            shape((local, fin), BF16),
            shape((SPAN, half, local), BF16),
            shape((local, half), F32),
            shape((local, 1), F32),
        ),
        in_specs=[VMEM, SMEM] + [VMEM] * 5,
        out_specs=(VMEM,) * 5,
        compiler_params=params(),
    )(all_tiles, all_cols, row_ids, band_ids, band, cots, output_weight)
    first_band, term_band = pl.pallas_call(
        functools.partial(band_kernel, rows),
        out_shape=(shape((SPAN, local, fin), BF16), shape((4, half, local), BF16)),
        in_specs=[VMEM] * 2,
        out_specs=(VMEM,) * 2,
        scratch_shapes=[pltpu.VMEM((2, half, local), BF16)] * 2 + sems(12),
        compiler_params=params(1),
    )(first, terms)
    second, grads = pl.pallas_call(
        functools.partial(back_kernel, reps),
        out_shape=(shape((local, half), BF16), shape((tall, half), F32)),
        in_specs=[VMEM] * 7,
        out_specs=(VMEM,) * 2,
        compiler_params=params(),
    )(dense, first_band, term_band, input_weight, own, degree, cots)
    second = second.reshape(reps, quarter, half)
    full = pl.pallas_call(
        functools.partial(swap_kernel, reps),
        out_shape=shape((reps, quarter, half), BF16),
        in_specs=[ANY],
        out_specs=ANY,
        scratch_shapes=sems(reps),
        compiler_params=params(2),
    )(second)
    whole = lax.all_gather(lax.psum(grads, "row"), "rep", axis=0)
    scores = dot(full.transpose(1, 0, 2).reshape(quarter, hid), output_weight, (1, 0)).astype(BF16)
    grad_input = whole[:, tall - fin:].transpose(1, 0, 2).reshape(fin, hid)
    grad_output = whole[:, :tall - fin].reshape(reps, hid // half, half, half)
    grad_output = grad_output.transpose(0, 2, 1, 3).reshape(hid, hid)
    return scores, grad_input, grad_output


def solution(mesh):
    placed = (
        P("row", None),
        P(),
        P(),
        P(("row", "rep"), None),
        P("row", "rep", None, None),
        P("row", "rep"),
        P(),
    )
    return jax.shard_map(
        body,
        mesh=mesh,
        in_specs=placed,
        out_specs=(P(("row", "rep"), None), P(), P()),
        check_vma=False,
    )
```

```python
import functools

import jax
import jax.numpy as jnp
from jax import lax
from jax.experimental import pallas as pl
from jax.experimental.pallas import tpu as pltpu
from jax.sharding import PartitionSpec as P

HOPS = 3
SPAN = 2 * HOPS + 1
MESH = pl.DeviceIdType.MESH
ANY = pl.BlockSpec(memory_space=pl.ANY)
HBM = pl.BlockSpec(memory_space=pltpu.HBM)
VMEM = pl.BlockSpec(memory_space=pltpu.VMEM)
SMEM = pl.BlockSpec(memory_space=pltpu.SMEM)
F32 = jnp.float32
BF16 = jnp.bfloat16


def dot(a, b, dims):
    return lax.dot_general(a, b, ((dims[:1], dims[1:]), ((), ())), preferred_element_type=F32)


def greet(peers):
    barrier = pltpu.get_barrier_semaphore()
    for peer in peers:
        pl.semaphore_signal(barrier, inc=1, device_id=peer, device_id_type=MESH)
    pl.semaphore_wait(barrier, len(peers))


def remote(src, dst, send, recv, index, peer):
    return pltpu.make_async_remote_copy(
        src_ref=src, dst_ref=dst, send_sem=send.at[index], recv_sem=recv.at[index],
        device_id=peer, device_id_type=MESH,
    )


def places(rows):
    row, rep = lax.axis_index("row"), lax.axis_index("rep")
    core = lax.rem(row, 2)
    flip, far = 1 - 2 * core, 6 * core - 3

    def at(shift):
        return (lax.rem(row + shift + rows, rows), rep)

    return flip, far, at


def start_rows(rows, src, band, send, recv, base):
    flip, far, at = places(rows)
    copies = [remote(src, band.at[HOPS - shift], send, recv, base + n, at(shift))
              for n, shift in enumerate((2, -2, far, flip))]
    for copy in copies:
        copy.start()
    return copies


def finish_rows(rows, copies, band, send, recv, base):
    flip, far, at = places(rows)
    passed = []
    for n, shift in enumerate((2, -2)):
        copies[n].wait_recv()
        step = remote(band.at[HOPS - shift], band.at[HOPS - shift - flip], send, recv, base + n, at(flip))
        step.start()
        passed.append(step)
    for copy in copies[2:]:
        copy.wait_recv()
    for copy in copies:
        copy.wait_send()
    for copy in passed:
        copy.wait()


def open_kernel(rows, reps, feats, cot, tiles, cols, band, cots, all_tiles, all_cols, send, recv, local):
    row, rep = lax.axis_index("row"), lax.axis_index("rep")
    flip, far, at = places(rows)
    others = [(row, lax.rem(rep + t, reps)) for t in range(1, reps)]
    greet([at(2), at(-2), at(far), at(flip)] + others)
    copies, n = [], 0
    pieces = ((tiles, all_tiles), (cols, all_cols), (cot, cots))
    pieces = pieces if cot is not None else pieces[:2]
    for peer in others:
        for src, dst in pieces:
            copies.append(remote(src, dst.at[rep], send, recv, n, peer))
            n += 1
    for i, (src, dst) in enumerate(pieces):
        copies.append(pltpu.make_async_copy(src, dst.at[rep], local.at[i]))
    copies.append(pltpu.make_async_copy(feats, band.at[HOPS], local.at[3]))
    for copy in copies:
        copy.start()
    moved = start_rows(rows, feats, band, send, recv, n)
    finish_rows(rows, moved, band, send, recv, n + 4)
    for copy in copies:
        copy.wait()


def scale_terms(rep, reps, cots, w2, dense, degree, terms):
    size = degree.shape[0]
    half = w2.shape[0] // reps
    at = pl.ds(pl.multiple_of(rep * half, half), half)
    pulled = dot(cots[...].reshape(size, -1), w2[at, :], (1, 1))
    scaled = (pulled / degree).astype(BF16)
    scaled_t = scaled.astype(F32).T.astype(BF16)
    for s in range(SPAN):
        part = dot(scaled_t, dense[:, s * size:(s + 1) * size], (1, 0))
        if s == HOPS:
            own = part.T + scaled.astype(F32)
        terms[s] = part.astype(BF16)
    return own


def share_kernel(rows, reps, feats, tiles, cols, band, all_tiles, all_cols, send, recv, local):
    open_kernel(rows, reps, feats, None, tiles, cols, band, None, all_tiles, all_cols, send, recv, local)


def front_kernel(rows, reps, blocks, tile, tiles, cols, row_ids, band_ids, band,
                 dense, first_o, deg_o):
    row = lax.axis_index("row")
    total = rows * blocks
    per = tiles.shape[2]
    dense[...] = jnp.zeros_like(dense)
    for b in range(blocks):
        at = pl.ds(b * tile, tile)
        ids = row_ids[at, :]
        sums = jnp.ones((tile, 1), F32)
        for j in range(reps):
            for k in range(per):
                slot = lax.rem(cols[j, b, k] + total - (row - HOPS) * blocks, total)
                same = ids == band_ids[pl.ds(slot, 1), :]
                value = jnp.where(same, tiles[j, b, k].astype(F32), 0.0)
                sums = sums + jnp.sum(value, axis=1, keepdims=True)
                dense[at, pl.ds(pl.multiple_of(slot * tile, tile), tile)] = value.astype(BF16)
        deg_o[at, :] = sums
    degree = deg_o[...]
    local = blocks * tile
    flat = band[...].reshape(SPAN * local, -1)
    summed = dot(dense[...], flat, (1, 0))
    first = ((summed + band[HOPS].astype(F32)) / degree).astype(BF16)
    first_o[...] = first


def full_front_kernel(rows, reps, blocks, tile, tiles, cols, row_ids, band_ids, band, cots, w2,
                      dense, first_o, terms_o, own_o, deg_o):
    front_kernel(rows, reps, blocks, tile, tiles, cols, row_ids, band_ids, band, dense, first_o, deg_o)
    own_o[...] = scale_terms(lax.axis_index("rep"), reps, cots, w2, dense, deg_o[...], terms_o)


def band_kernel(rows, first, terms, first_band, term_band, pair, joint, send, recv, local):
    flip, far, at = places(rows)
    greet([at(2), at(-2), at(far), at(flip)])
    joined = [remote(terms.at[HOPS + shift + flip], pair.at[n], send, recv, n, at(flip))
              for n, shift in enumerate((2, -2))]
    for copy in joined:
        copy.start()
    direct = [remote(terms.at[HOPS + far], term_band.at[2], send, recv, 2, at(far))]
    direct[0].start()
    moved = start_rows(rows, first, first_band, send, recv, 3)
    keep = pltpu.make_async_copy(first, first_band.at[HOPS], local.at[0])
    keep.start()
    direct.append(remote(terms.at[HOPS + flip], term_band.at[3], send, recv, 7, at(flip)))
    direct[1].start()
    for n, shift in enumerate((2, -2)):
        joined[n].wait_recv()
        joint[n] = (terms[HOPS + shift].astype(F32) + pair[n].astype(F32)).astype(BF16)
        step = remote(joint.at[n], term_band.at[n], send, recv, 8 + n, at(shift))
        step.start()
        direct.append(step)
    finish_rows(rows, moved, first_band, send, recv, 10)
    keep.wait()
    for copy in joined:
        copy.wait_send()
    for copy in direct:
        copy.wait()


def back_kernel(reps, dense, first_band, term_band, w1, own, deg, cots, second_o, grads_o):
    rep = lax.axis_index("rep")
    local, half = own.shape
    weight = w1[:, pl.ds(pl.multiple_of(rep * half, half), half)]
    preact = dot(first_band[HOPS], weight, (1, 0))
    mine = jnp.maximum(preact, 0.0).astype(BF16)
    summed = mine.astype(F32)
    for s in range(SPAN):
        hidden = mine if s == HOPS else jnp.maximum(dot(first_band[s], weight, (1, 0)), 0.0).astype(BF16)
        summed = summed + dot(dense[:, s * local:(s + 1) * local], hidden, (1, 0))
    second = (summed / deg[...]).astype(BF16)
    second_o[...] = second
    out = dot(second, cots[...].reshape(local, -1), (0, 0))
    width = out.shape[1] // half
    for i in range(width):
        grads_o[i * half:(i + 1) * half, :] = out[:, i * half:(i + 1) * half]
    got = term_band[0].astype(F32)
    for i in range(1, 4):
        got = got + term_band[i].astype(F32)
    back = got.T + own[...]
    delta = jnp.where(preact > 0.0, back, 0.0).astype(BF16)
    grads_o[width * half:, :] = dot(first_band[HOPS], delta, (0, 0))


def swap_kernel(reps, second, full, send, recv, local):
    row, rep = lax.axis_index("row"), lax.axis_index("rep")
    others = [(row, lax.rem(rep + t, reps)) for t in range(1, reps)]
    greet(others)
    copies = [remote(second.at[peer[1]], full.at[rep], send, recv, n, peer) for n, peer in enumerate(others)]
    copies.append(pltpu.make_async_copy(second.at[rep], full.at[rep], local.at[0]))
    for copy in copies:
        copy.start()
    for copy in copies:
        copy.wait()


def rest_kernel(rows, reps, first, dense, w1, w2, deg, cot, full, whole,
                cots, terms, first_band, term_band, pair, joint, second_s, go, gi, go_pair, gi_pair, go_mine, gi_mine,
                go_parts, gi_parts, send, recv, local):
    row, rep = lax.axis_index("row"), lax.axis_index("rep")
    flip, far, at = places(rows)
    chips = rows // 2
    chip, core = row // 2, lax.rem(row, 2)
    sibling = at(flip)
    turns = [lax.rem(chip + t, chips) for t in range(1, chips)]
    peers = [(q * 2 + core, rep) for q in turns]
    others = [(row, lax.rem(rep + t, reps)) for t in range(1, reps)]
    greet([sibling, at(far)] + peers + others)
    swaps = [remote(cot, cots.at[rep], send, recv, 12 + n, peer) for n, peer in enumerate(others)]
    swaps.append(pltpu.make_async_copy(cot, cots.at[rep], local.at[2]))
    for copy in swaps:
        copy.start()
    moved = start_rows(rows, first, first_band, send, recv, 3)
    keep = pltpu.make_async_copy(first, first_band.at[HOPS], local.at[0])
    keep.start()
    for copy in swaps:
        copy.wait()
    own = scale_terms(rep, reps, cots, w2, dense, deg[...], terms)
    joined = [remote(terms.at[HOPS + shift + flip], pair.at[n], send, recv, n, sibling)
              for n, shift in enumerate((2, -2))]
    for copy in joined:
        copy.start()
    direct = [remote(terms.at[HOPS + far], term_band.at[2], send, recv, 2, at(far))]
    direct[0].start()
    direct.append(remote(terms.at[HOPS + flip], term_band.at[3], send, recv, 7, sibling))
    direct[1].start()
    for n, shift in enumerate((2, -2)):
        joined[n].wait_recv()
        joint[n] = (terms[HOPS + shift].astype(F32) + pair[n].astype(F32)).astype(BF16)
        step = remote(joint.at[n], term_band.at[n], send, recv, 8 + n, at(shift))
        step.start()
        direct.append(step)
    finish_rows(rows, moved, first_band, send, recv, 10)
    keep.wait()

    size, half = own.shape
    weight = w1[:, pl.ds(pl.multiple_of(rep * half, half), half)]
    mine_first = first_band[HOPS]
    preact = dot(mine_first, weight, (1, 0))
    mine = jnp.maximum(preact, 0.0).astype(BF16)
    summed = mine.astype(F32)
    for s in range(SPAN):
        hidden = mine if s == HOPS else jnp.maximum(dot(first_band[s], weight, (1, 0)), 0.0).astype(BF16)
        summed = summed + dot(dense[:, s * size:(s + 1) * size], hidden, (1, 0))
    second = (summed / deg[...]).astype(BF16)
    second_s[...] = second.reshape(second_s.shape)
    base = 11 + reps
    late = [remote(second_s.at[peer[1]], full.at[rep], send, recv, base + n, peer) for n, peer in enumerate(others)]
    late.append(pltpu.make_async_copy(second_s.at[rep], full.at[rep], local.at[1]))
    for copy in late:
        copy.start()
    base = base + reps - 1
    out = dot(second, cots[...].reshape(size, -1), (0, 0))
    width = out.shape[1] // half
    out = jnp.concatenate([out[:, i * half:(i + 1) * half] for i in range(width)], axis=0)
    go[...] = out.reshape(go.shape)

    def fold(grads, got, total, parts, base):
        a = remote(grads.at[1 - core], got, send, recv, base, sibling)
        a.start()

        def rest():
            a.wait()
            total[...] = grads[core] + got[...]
            copies = [remote(total.at[q], parts.at[t], send, recv, base + 1 + t, peer)
                      for t, (q, peer) in enumerate(zip(turns, peers))]
            for copy in copies:
                copy.start()
            return copies

        return rest

    def gathered(copies, total, parts):
        value = total[chip]
        for t, copy in enumerate(copies):
            copy.wait_recv()
            value = value + parts[t]
        return value

    go_copies = fold(go, go_pair, go_mine, go_parts, base)()
    base = base + chips
    for copy in direct:
        copy.wait()
    got = term_band[0].astype(F32)
    for i in range(1, 4):
        got = got + term_band[i].astype(F32)
    back = got.T + own
    delta = jnp.where(preact > 0.0, back, 0.0).astype(BF16)
    gi[...] = dot(mine_first, delta, (0, 0)).reshape(gi.shape)
    rest = fold(gi, gi_pair, gi_mine, gi_parts, base)
    base = base + chips
    go_total = gathered(go_copies, go_mine, go_parts)
    gi_copies = rest()
    gi_total = gathered(gi_copies, gi_mine, gi_parts)
    whole[rep, core, chip] = jnp.concatenate([go_total, gi_total], axis=0).astype(BF16)
    spot = whole.at[rep, core, chip]
    spread = [remote(spot, spot, send, recv, base + t, peer) for t, peer in enumerate(peers)]
    for copy in spread:
        copy.start()
    base = base + chips - 1
    for copy in joined + go_copies + gi_copies:
        copy.wait_send()
    for copy in spread:
        copy.wait()
    block = whole.at[rep, core]
    last = [remote(block, block, send, recv, base + n, peer) for n, peer in enumerate(others)]
    base = base + reps - 1
    side = [remote(block, block, send, recv, base, sibling)]
    for copy in last + side:
        copy.start()
    for n, copy in enumerate(last):
        copy.wait_recv()
        came = whole.at[lax.rem(rep + reps - 1 - n, reps), core]
        step = remote(came, came, send, recv, base + 1 + n, sibling)
        step.start()
        side.append(step)
    for copy in last:
        copy.wait_send()
    for copy in side + late:
        copy.wait()


def close_kernel(deep, full, whole, w2, scores_o, gi_o, go_o):
    reps, half = full.shape[0], full.shape[2]
    for j in range(reps):
        at = slice(j * half, (j + 1) * half)
        part = dot(full[j], w2[at, :], (1, 0))
        total = part if j == 0 else total + part
        part = whole[j].astype(F32)
        gi_o[:, at] = part[..., deep:, :].reshape(gi_o.shape[0], half)
        part = part[..., :deep, :].reshape(-1, half)
        for i in range(part.shape[0] // half):
            go_o[at, i * half:(i + 1) * half] = part[i * half:(i + 1) * half]
    scores_o[...] = total.astype(BF16)


def params(number=None, limit=48 << 20):
    if number is None:
        return pltpu.CompilerParams(vmem_limit_bytes=limit)
    return pltpu.CompilerParams(vmem_limit_bytes=limit, collective_id=number, has_side_effects=True)


def shape(dims, kind):
    return jax.ShapeDtypeStruct(dims, kind)


def sems(count):
    return [pltpu.SemaphoreType.DMA((count,)), pltpu.SemaphoreType.DMA((count,)), pltpu.SemaphoreType.DMA((4,))]


def body(
    features, input_weight, output_weight, cotangent, adjacency_tiles, block_columns, graph_sizes
):
    row = lax.axis_index("row")
    rows, reps = lax.axis_size("row"), lax.axis_size("rep")
    blocks, per, tile = adjacency_tiles.shape[:3]
    local = blocks * tile
    fin = features.shape[1]
    hid = output_weight.shape[0]
    half, quarter = hid // reps, local // reps
    nodes = rows * local
    ends = jnp.cumsum(graph_sizes)

    def graph_of(places):
        return jnp.sum((places[..., None] >= ends).astype(jnp.int32), axis=-1)

    spots = lax.rem((row - HOPS) * local + nodes + jnp.arange(SPAN * local, dtype=jnp.int32), nodes)
    ids = graph_of(spots)
    row_ids = ids[HOPS * local:(HOPS + 1) * local].reshape(local, 1)
    band_ids = ids.reshape(SPAN * blocks, tile)
    padded = jnp.pad(block_columns, ((0, 8 - blocks), (0, 128 - per)))
    tall = hid * hid // reps // half + fin
    if 6 < rows <= 16 and rows % 2 == 0 and fin % (8 * rows) == 0:
        chips, deep, thin = rows // 2, hid // rows, fin // rows

        band, all_tiles, all_cols = pl.pallas_call(
            functools.partial(share_kernel, rows, reps),
            out_shape=(
                shape((SPAN, local, fin), BF16),
                shape((reps,) + adjacency_tiles.shape, BF16),
                shape((reps, 8, 128), jnp.int32),
            ),
            in_specs=[HBM] * 3,
            out_specs=(VMEM,) * 2 + (ANY,),
            scratch_shapes=sems(2 * (reps - 1) + 6),
            compiler_params=params(0),
        )(features, adjacency_tiles, padded)
        dense, first, degree = pl.pallas_call(
            functools.partial(front_kernel, rows, reps, blocks, tile),
            out_shape=(
                shape((local, SPAN * local), BF16),
                shape((local, fin), BF16),
                shape((local, 1), F32),
            ),
            in_specs=[VMEM, SMEM] + [VMEM] * 3,
            out_specs=(VMEM,) * 3,
            compiler_params=params(),
        )(all_tiles, all_cols, row_ids, band_ids, band)

        def bank(*dims):
            return pltpu.VMEM(dims, F32)

        full, whole = pl.pallas_call(
            functools.partial(rest_kernel, rows, reps),
            out_shape=(
                shape((reps, quarter, half), BF16),
                shape((reps, 2, chips, deep + thin, half), BF16),
            ),
            in_specs=[VMEM] * 6,
            out_specs=(VMEM,) * 2,
            scratch_shapes=[
                pltpu.VMEM((reps, quarter, hid), BF16),
                pltpu.VMEM((SPAN, half, local), BF16),
                pltpu.VMEM((SPAN, local, fin), BF16),
                pltpu.VMEM((4, half, local), BF16),
                pltpu.VMEM((2, half, local), BF16),
                pltpu.VMEM((2, half, local), BF16),
                pltpu.VMEM((reps, quarter, half), BF16),
                bank(2, chips, deep, half),
                bank(2, chips, thin, half),
                bank(chips, deep, half),
                bank(chips, thin, half),
                bank(chips, deep, half),
                bank(chips, thin, half),
                bank(chips - 1, deep, half),
                bank(chips - 1, thin, half),
            ] + sems(12 + 4 * reps + 3 * chips),
            compiler_params=params(1, 60 << 20),
        )(first, dense, input_weight, output_weight, degree, cotangent)
        scores, grad_input, grad_output = pl.pallas_call(
            functools.partial(close_kernel, deep),
            out_shape=(shape((quarter, hid), BF16), shape((fin, hid), F32), shape((hid, hid), F32)),
            in_specs=[VMEM] * 3,
            out_specs=(VMEM,) * 3,
            compiler_params=params(),
        )(full, whole, output_weight)
        return scores, grad_input, grad_output
    band, cots, all_tiles, all_cols = pl.pallas_call(
        functools.partial(open_kernel, rows, reps),
        out_shape=(
            shape((SPAN, local, fin), BF16),
            shape((reps, quarter, hid), BF16),
            shape((reps,) + adjacency_tiles.shape, BF16),
            shape((reps, 8, 128), jnp.int32),
        ),
        in_specs=[HBM] * 4,
        out_specs=(VMEM,) * 3 + (ANY,),
        scratch_shapes=sems(3 * (reps - 1) + 6),
        compiler_params=params(0),
    )(features, cotangent, adjacency_tiles, padded)
    dense, first, terms, own, degree = pl.pallas_call(
        functools.partial(full_front_kernel, rows, reps, blocks, tile),
        out_shape=(
            shape((local, SPAN * local), BF16),
            shape((local, fin), BF16),
            shape((SPAN, half, local), BF16),
            shape((local, half), F32),
            shape((local, 1), F32),
        ),
        in_specs=[VMEM, SMEM] + [VMEM] * 5,
        out_specs=(VMEM,) * 5,
        compiler_params=params(),
    )(all_tiles, all_cols, row_ids, band_ids, band, cots, output_weight)
    first_band, term_band = pl.pallas_call(
        functools.partial(band_kernel, rows),
        out_shape=(shape((SPAN, local, fin), BF16), shape((4, half, local), BF16)),
        in_specs=[VMEM] * 2,
        out_specs=(VMEM,) * 2,
        scratch_shapes=[pltpu.VMEM((2, half, local), BF16)] * 2 + sems(12),
        compiler_params=params(1),
    )(first, terms)
    second, grads = pl.pallas_call(
        functools.partial(back_kernel, reps),
        out_shape=(shape((local, half), BF16), shape((tall, half), F32)),
        in_specs=[VMEM] * 7,
        out_specs=(VMEM,) * 2,
        compiler_params=params(),
    )(dense, first_band, term_band, input_weight, own, degree, cots)
    second = second.reshape(reps, quarter, half)
    full = pl.pallas_call(
        functools.partial(swap_kernel, reps),
        out_shape=shape((reps, quarter, half), BF16),
        in_specs=[ANY],
        out_specs=ANY,
        scratch_shapes=sems(reps),
        compiler_params=params(2),
    )(second)
    whole = lax.all_gather(lax.psum(grads, "row"), "rep", axis=0)
    scores = dot(full.transpose(1, 0, 2).reshape(quarter, hid), output_weight, (1, 0)).astype(BF16)
    grad_input = whole[:, tall - fin:].transpose(1, 0, 2).reshape(fin, hid)
    grad_output = whole[:, :tall - fin].reshape(reps, hid // half, half, half)
    grad_output = grad_output.transpose(0, 2, 1, 3).reshape(hid, hid)
    return scores, grad_input, grad_output


def solution(mesh):
    placed = (
        P("row", None),
        P(),
        P(),
        P(("row", "rep"), None),
        P("row", "rep", None, None),
        P("row", "rep"),
        P(),
    )
    return jax.shard_map(
        body,
        mesh=mesh,
        in_specs=placed,
        out_specs=(P(("row", "rep"), None), P(), P()),
        check_vma=False,
    )
```
